32 devices in a mesh: grp: 2 (over y), row: 4 (over z), col: 4 (over x, core).
Axes of the slice: x: 2, y: 2, z: 4, core: 2. Of those that a mesh axis runs over, the one named last changes fastest.
Arguments:
- mask_param: float32 [2048, 1024], P(('grp', 'row'), 'col'), parts along dimension 0, may hold values from -6 to 6
- target: bfloat16 [2048, 1024], P(('grp', 'row'), 'col'), parts along dimension 0, may hold values from 0 to 1
- kernel_modes: float32 [12, 64, 128], replicated, may hold values from -24 to 24, as said below
- kernel_weight: float32 [12], replicated, may hold values from 0.02 to 0.2
Outputs:
- healed_param: float32 [2048, 1024], P(('grp', 'row'), 'col'), parts along dimension 0
The draws below stay inside these ranges and needn't reach their ends.
There are 2 independent parts, one for each index of `grp`. The reference program is written for one: setup_inputs(seed, part) draws one part's arguments, and reference() takes and returns one part's arrays. A program takes and returns all parts, laid end to end along the dimension named above; an argument that names none is the same for every part. Nothing has to cross between parts.
Inputs may be any that keep to these rules, and one draw needn't show every extreme that they name: `kernel_modes`: the response of every kernel at the zero-frequency mode (row 32, columns 32 and 96) is zero.
All inputs are finite; a program needn't handle non-finite values.
Results may differ from the reference program's by a relative error of at most 0.0095.
Values may be sent and summed in bfloat16 or wider, within the bound.
No kernel may reach another device: no remote copies, remote signals or barrier semaphores. Data moves between devices by JAX's collectives and lax.ppermute only.
A program may use at most 64 MiB of HBM per device.

```python
import math
import jax
import jax.numpy as jnp
from jax import lax

TILE = 256
MARGIN = 64
MODES = 64
KERN = 12
HALF = 128
WIN = 384
ROWS = 1024
COLS = 1024
N_ROW = 4
N_COL = 4


def draw_kernel_modes(key, part):
    shape = (KERN, MODES, 2 * MODES)
    base = jnp.clip(jax.random.normal(key, shape, jnp.float32), -6.0, 6.0)
    level = 0.6 * WIN / MODES
    rows_idx = jnp.arange(MODES, dtype=jnp.int32)[:, None]
    cols_idx = jnp.arange(2 * MODES, dtype=jnp.int32)[None, :]
    centre = (rows_idx == MODES // 2) & (jnp.mod(cols_idx, MODES) == MODES // 2)
    return jnp.where(centre[None], 0.0, level * base).astype(jnp.float32)


def level_of(rng, extent, cuts, low, largest):
    def one(axis_at, shards_of):
        heights = jax.random.uniform(jax.random.fold_in(jax.random.fold_in(rng, 6), axis_at), (shards_of,), jnp.float32, low / len(cuts), largest / len(cuts))
        return jnp.repeat(jnp.exp(heights), extent[axis_at] // shards_of).reshape((-1,) + (1,) * (len(extent) - axis_at - 1))

    loudness = one(*cuts[0])
    for cut in cuts[1:]:
        loudness = loudness * one(*cut)
    return loudness


def bell_draw(own_key, shape, deviation, most, cuts=(), held_as=jnp.bfloat16):
    drawn = deviation * jax.random.normal(own_key, shape, jnp.float32)
    if cuts:
        drawn = drawn * level_of(own_key, shape, cuts, -0.22, 0.18)
    return jnp.clip(drawn, -most, most).astype(held_as)


def setup_inputs(seed: int = 0, part: int = 0) -> dict:
    key_list = jax.random.split(jax.random.key(seed), 5)
    part_keys = jax.random.split(jax.random.fold_in(key_list[4], part), 5)
    mask_param = bell_draw(part_keys[0], (ROWS, COLS), 1.5, 6.0, ((0, 4), (1, 4)), jnp.float32)
    target = jnp.clip(1.0 * jax.random.uniform(part_keys[1], (ROWS, COLS), jnp.float32) ** level_of(part_keys[1], (ROWS, COLS), ((0, 4), (1, 4)), -0.2, 0.2), 0.0, 1.0).astype(jnp.bfloat16)
    kernel_modes = draw_kernel_modes(jax.random.fold_in(key_list[4], 71), part)
    kernel_weight = jnp.clip(jnp.exp(jax.random.uniform(key_list[3], (KERN,), jnp.float32, math.log(0.02), math.log(0.2))), 0.02, 0.2)
    return {"mask_param": mask_param, "target": target, "kernel_modes": kernel_modes, "kernel_weight": kernel_weight}


steepness = 4.0
threshold = 0.4
step_rate = 16.0


def dft_tables():
    frequency = jnp.arange(MODES, dtype=jnp.int32) - MODES // 2
    places = jnp.arange(WIN, dtype=jnp.int32)
    phase_index = jnp.mod(frequency[:, None] * places[None, :], WIN)
    phase_angle = phase_index.astype(jnp.float32) * (2.0 * math.pi / WIN)
    cos_table = jnp.cos(phase_angle).astype(jnp.bfloat16)
    sin_table = jnp.sin(phase_angle).astype(jnp.bfloat16)
    stacked = jnp.concatenate([cos_table, sin_table], axis=0)
    forward_table = jnp.concatenate([cos_table.T, sin_table.T], axis=1)
    inverse_table = jnp.concatenate([jnp.concatenate([cos_table, sin_table], 1), jnp.concatenate([-sin_table, cos_table], 1)], 0)
    adjoint_table = jnp.concatenate([jnp.concatenate([cos_table.T, -sin_table.T], 1), jnp.concatenate([sin_table.T, cos_table.T], 1)], 0)
    return stacked, forward_table, inverse_table, adjoint_table


def window_gradient(window_mask, target_core, weight_core, kernel_modes, kernel_weight):
    stacked, forward_table, inverse_table, adjoint_table = dft_tables()
    half_spec = jnp.dot(window_mask, forward_table, preferred_element_type=jnp.float32).astype(jnp.bfloat16)
    blocks = jnp.dot(stacked, half_spec, preferred_element_type=jnp.float32)
    spec_real = (blocks[:MODES, :MODES] - blocks[MODES:, MODES:]) / (WIN * WIN)
    spec_imag = -(blocks[:MODES, MODES:] + blocks[MODES:, :MODES]) / (WIN * WIN)

    def field_of(kernel_index):
        kernel_one = kernel_modes[kernel_index]
        resp_real = kernel_one[:, :MODES]
        resp_imag = kernel_one[:, MODES:]
        filtered = jnp.concatenate([resp_real * spec_real - resp_imag * spec_imag, resp_real * spec_imag + resp_imag * spec_real], 1).astype(jnp.bfloat16)
        partial_value = jnp.dot(filtered, inverse_table, preferred_element_type=jnp.float32).astype(jnp.bfloat16)
        field_real = partial_value[:, :WIN]
        field_imag = partial_value[:, WIN:]
        rotated = jnp.concatenate([jnp.concatenate([field_real, field_imag], 1), jnp.concatenate([-field_imag, field_real], 1)], 0)
        return jnp.dot(stacked.T, rotated, preferred_element_type=jnp.float32), resp_real, resp_imag

    def add_intensity(running, kernel_index):
        field_pair, resp_real, resp_imag = field_of(kernel_index)
        field_power = field_pair[:, :WIN] * field_pair[:, :WIN] + field_pair[:, WIN:] * field_pair[:, WIN:]
        return running + kernel_weight[kernel_index] * field_power, None

    kernel_ids = jnp.arange(KERN, dtype=jnp.int32)
    intensity, _ = lax.scan(add_intensity, jnp.zeros((WIN, WIN), jnp.float32), kernel_ids)
    core_level = intensity[MARGIN:MARGIN + TILE, MARGIN:MARGIN + TILE]
    printed = jax.nn.sigmoid(steepness * (core_level - threshold))
    core_grad = 2.0 * (printed - target_core.astype(jnp.float32)) * printed * (1.0 - printed) * steepness * weight_core
    grad_full = jnp.pad(core_grad, MARGIN)
    grad_both = jnp.concatenate([grad_full, grad_full], 1)

    def add_adjoint(running, kernel_index):
        field_pair, resp_real, resp_imag = field_of(kernel_index)
        scaled = (field_pair * grad_both * (2.0 * kernel_weight[kernel_index])).astype(jnp.bfloat16)
        half_back = jnp.dot(scaled, adjoint_table, preferred_element_type=jnp.float32).astype(jnp.bfloat16)
        back_modes = jnp.dot(stacked, half_back, preferred_element_type=jnp.float32)
        back_real = back_modes[:MODES, :MODES] + back_modes[MODES:, MODES:]
        back_imag = back_modes[:MODES, MODES:] - back_modes[MODES:, :MODES]
        return (running[0] + resp_real * back_real + resp_imag * back_imag, running[1] + resp_real * back_imag - resp_imag * back_real), None

    zero_modes = jnp.zeros((MODES, MODES), jnp.float32)
    (acc_real, acc_imag), _ = lax.scan(add_adjoint, (zero_modes, zero_modes), kernel_ids)
    combined = jnp.concatenate([acc_real, acc_imag], 1).astype(jnp.bfloat16)
    partial_back = jnp.dot(combined, inverse_table, preferred_element_type=jnp.float32).astype(jnp.bfloat16)
    stacked_back = jnp.concatenate([partial_back[:, :WIN], -partial_back[:, WIN:]], 0)
    mask_grad = jnp.dot(stacked.T, stacked_back, preferred_element_type=jnp.float32) / (WIN * WIN)
    return mask_grad[MARGIN:MARGIN + TILE, MARGIN:MARGIN + TILE]


def tile_join(pieces):
    return pieces.reshape(N_ROW, N_COL, TILE, TILE).transpose(0, 2, 1, 3).reshape(ROWS, COLS)


def reference(mask_param, target, kernel_modes, kernel_weight):
    tile_ids = jnp.arange(N_ROW * N_COL, dtype=jnp.int32)
    soft_mask = jax.nn.sigmoid(mask_param)
    wire_mask = soft_mask.astype(jnp.bfloat16)
    padded = jnp.pad(wire_mask, MARGIN)
    unit_weight = jnp.ones((TILE, TILE), jnp.float32)

    def first_update(tile_index):
        row_start = (tile_index // N_COL) * TILE
        col_start = (tile_index % N_COL) * TILE
        window = lax.dynamic_slice(padded, (row_start, col_start), (WIN, WIN))
        goal_tile = lax.dynamic_slice(target, (row_start, col_start), (TILE, TILE))
        own_soft = lax.dynamic_slice(soft_mask, (row_start, col_start), (TILE, TILE))
        mask_grad = window_gradient(window, goal_tile, unit_weight, kernel_modes, kernel_weight)
        return mask_grad * own_soft * (1.0 - own_soft)

    first_param = mask_param - step_rate * tile_join(lax.map(first_update, tile_ids))
    wire_first = jax.nn.sigmoid(first_param).astype(jnp.bfloat16)
    pad_extra = HALF + MARGIN
    padded_first = jnp.pad(wire_first, ((0, pad_extra), (0, pad_extra)))
    first_padded = jnp.pad(first_param, ((0, HALF), (0, HALF)))
    target_padded = jnp.pad(target, ((0, HALF), (0, HALF)))
    core_place = jnp.arange(TILE, dtype=jnp.int32)

    def second_update(tile_index):
        row_start = (tile_index // N_COL) * TILE
        col_start = (tile_index % N_COL) * TILE
        window = lax.dynamic_slice(padded_first, (row_start + HALF - MARGIN, col_start + HALF - MARGIN), (WIN, WIN))
        goal_tile = lax.dynamic_slice(target_padded, (row_start + HALF, col_start + HALF), (TILE, TILE))
        core_param = lax.dynamic_slice(first_padded, (row_start + HALF, col_start + HALF), (TILE, TILE))
        rows_in = row_start + HALF + core_place < ROWS
        cols_in = col_start + HALF + core_place < COLS
        weight_core = (rows_in[:, None] & cols_in[None, :]).astype(jnp.float32)
        mask_grad = window_gradient(window, goal_tile, weight_core, kernel_modes, kernel_weight)
        core_soft = jax.nn.sigmoid(core_param)
        return core_param - step_rate * (mask_grad * core_soft * (1.0 - core_soft))

    new_cores = tile_join(lax.map(second_update, tile_ids))
    return first_param.at[HALF:, HALF:].set(new_cores[:ROWS - HALF, :COLS - HALF])
```

```python
import math

import jax
import jax.numpy as jnp
import numpy as np
from jax import lax
from jax.experimental import pallas as pl
from jax.experimental.pallas import tpu as pltpu
from jax.sharding import PartitionSpec as P

TILE = 256
MARGIN = 64
MODES = 64
KERN = 12
HALF = 128
WIN = 384
COARSE = 128
STEP = WIN // COARSE

steepness = 4.0
threshold = 0.4
step_rate = 16.0
area = float(WIN * WIN)

VMEM = pltpu.VMEM
BF16 = jnp.bfloat16
F32 = jnp.float32


def tables():
    freq = np.arange(MODES) - MODES // 2
    angle = (2.0 * math.pi / WIN) * np.mod(freq[:, None] * np.arange(WIN)[None], WIN)
    cos, sin = np.cos(angle), np.sin(angle)
    stacked = np.concatenate([cos, sin], 0)
    forward = stacked.T
    core = slice(MARGIN, MARGIN + TILE)
    c_core, s_core = cos[:, core], sin[:, core]
    c_low, s_low = cos[:, ::STEP], sin[:, ::STEP]
    reach = HALF + MARGIN
    place_a = np.zeros((TILE, 2 * MODES))
    place_a[TILE - reach :] = forward[:reach]
    place_b = np.zeros((TILE, 2 * MODES))
    place_b[:reach] = forward[reach:]
    offset = np.arange(MARGIN, MARGIN + TILE)[:, None] - STEP * np.arange(COARSE)[None]
    orders = np.arange(1, 2 * MODES // 2)
    interp = 1.0 + 2.0 * np.cos((2.0 * math.pi / WIN) * orders[:, None, None] * offset[None]).sum(0)
    interp = (interp + np.cos((2.0 * math.pi / WIN) * MODES * offset)) / COARSE
    high = interp.astype(jnp.bfloat16).astype(np.float64)
    table = dict(
        own=forward[core],
        rim=np.concatenate([forward[MARGIN + TILE :], forward[:MARGIN]], 0),
        q_own=stacked[:, core],
        q_rim=np.concatenate([stacked[:, :MARGIN], stacked[:, MARGIN + TILE :]], 1),
        spread=np.block([[c_low, s_low], [-s_low, c_low]]),
        q_low=np.concatenate([c_low.T, s_low.T], 1),
        interp=np.concatenate([high, interp - high], 1),
        interp_t=np.concatenate([high.T, (interp - high).T], 0),
        interp_h=high,
        interp_ht=high.T,
        gather=np.block(
            [[c_low.T, -s_low.T, -s_low.T, -c_low.T], [s_low.T, c_low.T, c_low.T, -s_low.T]]
        ),
        q_back=np.concatenate([c_low, s_low], 1),
        inverse=np.block([[c_core, s_core], [-s_core, c_core]]),
        q_inv=np.concatenate([c_core.T, -s_core.T], 1),
        place=np.concatenate([place_a, place_b], 1),
        q_place=np.concatenate([place_a.T, place_b.T], 0),
        inv_left=np.block([[c_core[:, HALF:], s_core[:, HALF:]], [-s_core[:, HALF:], c_core[:, HALF:]]]),
        inv_right=np.block([[c_core[:, :HALF], s_core[:, :HALF]], [-s_core[:, :HALF], c_core[:, :HALF]]]),
    )
    return {name: value.astype(jnp.bfloat16) for name, value in table.items()}


def dot(left, right):
    return jnp.dot(left, right, preferred_element_type=F32)


def swap_halves(value):
    return pltpu.roll(value, MODES, axis=1)


def low_lanes(shape):
    return lax.broadcasted_iota(jnp.int32, shape, 1) < MODES


def modes_of(blocks):
    top, bottom = blocks[:MODES], swap_halves(blocks[MODES:])
    return jnp.where(low_lanes(top.shape), top - bottom, -(top + bottom)) / area


def imaging_modes(spec, goal, weight, modes_ref, weight_ref, field_ref, grad_ref, t):
    swapped = swap_halves(spec)
    low = low_lanes(spec.shape)
    spec_a = jnp.where(low, spec, swapped)
    spec_b = jnp.where(low, -swapped, spec)
    filtered = []
    for k in range(KERN):
        resp = modes_ref[k]
        filtered.append((resp * spec_a + swap_halves(resp) * spec_b).astype(BF16))
    partial = dot(jnp.concatenate(filtered, 0), t["spread"][...]).astype(BF16)
    level = jnp.zeros((COARSE, COARSE), F32)
    for k in range(KERN):
        part = partial[k * MODES : (k + 1) * MODES]
        real, imag = part[:, :COARSE], part[:, COARSE:]
        rotated = jnp.concatenate([part, jnp.concatenate([-imag, real], 1)], 0)
        field = dot(t["q_low"][...], rotated)
        field_ref[k] = field
        a_real, a_imag = field[:, :COARSE], field[:, COARSE:]
        level = level + weight_ref[k] * (a_real * a_real + a_imag * a_imag)
    level = level.astype(BF16)
    half = dot(t["interp"][...], jnp.concatenate([level, level], 0)).astype(BF16)
    core = dot(jnp.concatenate([half, half], 1), t["interp_t"][...])
    printed = jax.nn.sigmoid(steepness * (core - threshold))
    core_grad = 2.0 * (printed - goal.astype(F32)) * printed * (1.0 - printed) * steepness
    if weight is not None:
        core_grad = jnp.where(weight, core_grad, 0.0)
    low_grad = dot(t["interp_ht"][...], core_grad.astype(BF16)).astype(BF16)
    low_grad = dot(low_grad, t["interp_h"][...])
    both = jnp.concatenate([low_grad, low_grad], 1)
    for k in range(KERN):
        scaled = field_ref[k] * both * (2.0 * weight_ref[k])
        grad_ref[k * COARSE : (k + 1) * COARSE, :] = scaled.astype(BF16)
    gathered = dot(grad_ref[...], t["gather"][...]).astype(BF16)
    direct = jnp.zeros((MODES, 2 * MODES), F32)
    crossed = jnp.zeros((MODES, 2 * MODES), F32)
    for k in range(KERN):
        rows = gathered[k * COARSE : (k + 1) * COARSE]
        back = dot(t["q_back"][...], jnp.concatenate([rows[:, :COARSE], rows[:, COARSE:]], 0))
        resp = modes_ref[k]
        direct = direct + resp * back
        crossed = crossed + swap_halves(resp) * back
    return jnp.where(low, direct + swap_halves(direct), crossed - swap_halves(crossed)).astype(BF16)


def edges_kernel(mask_ref, out_ref):
    wire = jax.nn.sigmoid(mask_ref[...])
    out_ref[...] = jnp.concatenate([wire[:, :MARGIN], wire[:, TILE - MARGIN :]], 1).astype(BF16)


def strip_kernel(cols, mask_ref, left_ref, right_ref, own_ref, rim_ref, u_ref, top_ref, bottom_ref):
    col = lax.axis_index("col")
    wire = jax.nn.sigmoid(mask_ref[...]).astype(BF16)
    low = low_lanes((TILE, 2 * MARGIN))
    keep = jnp.logical_or(
        jnp.logical_and(low, col < cols - 1), jnp.logical_and(jnp.logical_not(low), col > 0)
    )
    rim = jnp.where(low, right_ref[...].astype(F32), left_ref[...].astype(F32))
    rim = jnp.where(keep, rim, 0.0).astype(BF16)
    half_spec = (dot(wire, own_ref[...]) + dot(rim, rim_ref[...])).astype(BF16)
    u_ref[...] = half_spec
    top_ref[...] = half_spec[:MARGIN]
    bottom_ref[...] = half_spec[TILE - MARGIN :]


FIRST_TABLES = (
    "q_own", "q_rim", "spread", "q_low", "interp", "interp_t", "interp_h", "interp_ht",
    "gather", "q_back", "inverse", "q_inv", "place", "q_place",
)


def first_kernel(rows, *refs):
    mask_ref, u_ref, above_ref, below_ref, goal_ref, modes_ref, weight_ref = refs[:7]
    t = dict(zip(FIRST_TABLES, refs[7 : 7 + len(FIRST_TABLES)]))
    first_ref, aa_ref, ab_ref, ba_ref, bb_ref, field_ref, grad_ref = refs[7 + len(FIRST_TABLES) :]
    row = lax.axis_index("row")
    above = jnp.where(row > 0, above_ref[...].astype(F32), 0.0)
    below = jnp.where(row < rows - 1, below_ref[...].astype(F32), 0.0)
    rim = jnp.concatenate([above, below], 0).astype(BF16)
    spec = modes_of(dot(t["q_own"][...], u_ref[...]) + dot(t["q_rim"][...], rim))
    combined = imaging_modes(
        spec, goal_ref[...], None, modes_ref, weight_ref, field_ref, grad_ref, t
    )
    back = dot(combined, t["inverse"][...]).astype(BF16)
    mask_grad = dot(t["q_inv"][...], jnp.concatenate([back[:, :TILE], back[:, TILE:]], 0)) / area
    mask = mask_ref[...]
    soft = jax.nn.sigmoid(mask)
    first = mask - step_rate * (mask_grad * soft * (1.0 - soft))
    first_ref[...] = first
    wire = jax.nn.sigmoid(first).astype(BF16)
    half = dot(wire, t["place"][...])
    half_hi = half.astype(BF16)
    half_lo = (half - half_hi.astype(F32)).astype(BF16)
    blocks = dot(t["q_place"][...], half_hi) + dot(t["q_place"][...], half_lo)
    aa_ref[...] = modes_of(blocks[:HALF, :HALF])
    ab_ref[...] = modes_of(blocks[:HALF, HALF:])
    ba_ref[...] = modes_of(blocks[HALF:, :HALF])
    bb_ref[...] = modes_of(blocks[HALF:, HALF:])


HEAL_TABLES = (
    "spread", "q_low", "interp", "interp_t", "interp_h", "interp_ht", "gather", "q_back",
)


def heal_kernel(rows, cols, *refs):
    own_ref, right_ref, below_ref, corner_ref = refs[:4]
    goal_ref, goal_right_ref, goal_below_ref, modes_ref, weight_ref = refs[4:9]
    t = dict(zip(HEAL_TABLES, refs[9 : 9 + len(HEAL_TABLES)]))
    out_ref, field_ref, grad_ref = refs[9 + len(HEAL_TABLES) :]
    inner_row = lax.axis_index("row") < rows - 1
    inner_col = lax.axis_index("col") < cols - 1
    spec = own_ref[...]
    spec = spec + jnp.where(inner_col, right_ref[...], 0.0)
    spec = spec + jnp.where(inner_row, below_ref[...], 0.0)
    spec = spec + jnp.where(jnp.logical_and(inner_row, inner_col), corner_ref[...], 0.0)
    upper = jnp.concatenate([goal_ref[HALF:, HALF:], goal_right_ref[HALF:, :]], 1)
    goal = jnp.concatenate([upper, goal_below_ref[...]], 0)
    shape = (TILE, TILE)
    weight = jnp.logical_and(
        jnp.logical_or(lax.broadcasted_iota(jnp.int32, shape, 0) < HALF, inner_row),
        jnp.logical_or(lax.broadcasted_iota(jnp.int32, shape, 1) < HALF, inner_col),
    )
    out_ref[...] = imaging_modes(
        spec, goal, weight, modes_ref, weight_ref, field_ref, grad_ref, t
    )


def final_kernel(first_ref, own_ref, left_ref, up_ref, corner_ref, inv_left_ref, inv_right_ref, q_inv_ref, out_ref):
    has_row = lax.axis_index("row") > 0
    has_col = lax.axis_index("col") > 0

    def kept(ref, flag):
        return jnp.where(flag, ref[...].astype(F32), 0.0).astype(BF16)

    left = jnp.concatenate(
        [kept(left_ref, has_col), kept(corner_ref, jnp.logical_and(has_row, has_col))], 0
    )
    right = jnp.concatenate([own_ref[...], kept(up_ref, has_row)], 0)
    left = dot(left, inv_left_ref[...]).astype(BF16)
    right = dot(right, inv_right_ref[...]).astype(BF16)

    def quarter(rows):
        real = jnp.concatenate([left[rows, :HALF], right[rows, :HALF]], 1)
        imag = jnp.concatenate([left[rows, HALF:], right[rows, HALF:]], 1)
        return jnp.concatenate([real, imag], 0)

    lower = dot(q_inv_ref[:HALF, :], quarter(slice(0, MODES)))
    upper = dot(q_inv_ref[HALF:, :], quarter(slice(MODES, 2 * MODES)))
    grad = jnp.concatenate([upper, lower], 0) / area
    first = first_ref[...]
    soft = jax.nn.sigmoid(first)
    out_ref[...] = first - step_rate * (grad * soft * (1.0 - soft))


def vmem(count):
    return [pl.BlockSpec(memory_space=VMEM)] * count


SMEM_SPEC = pl.BlockSpec(memory_space=pltpu.SMEM)
FIELD_SCRATCH = [VMEM((KERN, COARSE, 2 * COARSE), F32), VMEM((KERN * COARSE, 2 * COARSE), BF16)]


def shape_of(rows, cols, dtype):
    return jax.ShapeDtypeStruct((rows, cols), dtype)


def per_device(rows, cols, mask_param, target, kernel_modes, kernel_weight):
    table = {name: jnp.asarray(value) for name, value in tables().items()}

    def move(value, down, right):
        pairs = [
            (r * cols + c, ((r + down) % rows) * cols + (c + right) % cols)
            for r in range(rows)
            for c in range(cols)
        ]
        return lax.ppermute(value, ("row", "col"), pairs)

    edges = pl.pallas_call(
        edges_kernel, out_shape=shape_of(TILE, 2 * MARGIN, BF16), in_specs=vmem(1),
        out_specs=vmem(1)[0], name="edges",
    )(mask_param)
    from_left = move(edges, 0, 1)
    from_right = move(edges, 0, -1)
    goal_right = move(target[:, :HALF], 0, -1)
    half_spec, top, bottom = pl.pallas_call(
        lambda *refs: strip_kernel(cols, *refs),
        out_shape=(
            shape_of(TILE, 2 * MODES, BF16), shape_of(MARGIN, 2 * MODES, BF16),
            shape_of(MARGIN, 2 * MODES, BF16),
        ),
        in_specs=vmem(5), out_specs=tuple(vmem(3)), name="strip",
    )(mask_param, from_left, from_right, table["own"], table["rim"])
    above = move(bottom, 1, 0)
    below = move(top, -1, 0)
    goal_below = move(jnp.concatenate([target[:HALF, HALF:], goal_right[:HALF]], 1), -1, 0)
    modes_shape = shape_of(MODES, 2 * MODES, F32)
    first, own, to_left, to_up, to_corner = pl.pallas_call(
        lambda *refs: first_kernel(rows, *refs),
        out_shape=(shape_of(TILE, TILE, F32),) + (modes_shape,) * 4,
        in_specs=vmem(6) + [SMEM_SPEC] + vmem(len(FIRST_TABLES)), out_specs=tuple(vmem(5)),
        scratch_shapes=FIELD_SCRATCH, name="first",
    )(
        mask_param, half_spec, above, below, target, kernel_modes, kernel_weight,
        *[table[name] for name in FIRST_TABLES],
    )
    spec_right = move(to_left, 0, -1)
    spec_below = move(to_up, -1, 0)
    spec_corner = move(to_corner, -1, -1)
    combined = pl.pallas_call(
        lambda *refs: heal_kernel(rows, cols, *refs),
        out_shape=shape_of(MODES, 2 * MODES, BF16),
        in_specs=vmem(8) + [SMEM_SPEC] + vmem(len(HEAL_TABLES)), out_specs=vmem(1)[0],
        scratch_shapes=FIELD_SCRATCH, name="heal",
    )(
        own, spec_right, spec_below, spec_corner, target, goal_right, goal_below,
        kernel_modes, kernel_weight, *[table[name] for name in HEAL_TABLES],
    )
    mode_left = move(combined, 0, 1)
    mode_up = move(combined, 1, 0)
    mode_corner = move(combined, 1, 1)
    return pl.pallas_call(
        final_kernel, out_shape=shape_of(TILE, TILE, F32), in_specs=vmem(8),
        out_specs=vmem(1)[0], name="final",
    )(
        first, combined, mode_left, mode_up, mode_corner,
        table["inv_left"], table["inv_right"], table["q_inv"],
    )


def solution(mesh):
    rows, cols = mesh.shape["row"], mesh.shape["col"]
    tile = P(("grp", "row"), "col")
    return jax.shard_map(
        lambda *args: per_device(rows, cols, *args), mesh=mesh,
        in_specs=(tile, tile, P(), P()), out_specs=tile, check_vma=False,
    )
```

```python
import math

import jax
import jax.numpy as jnp
import numpy as np
from jax import lax
from jax.experimental import pallas as pl
from jax.experimental.pallas import tpu as pltpu
from jax.sharding import PartitionSpec as P

TILE = 256
MARGIN = 64
MODES = 64
KERN = 12
HALF = 128
WIN = 384
COARSE = 128
STEP = WIN // COARSE

steepness = 4.0
threshold = 0.4
step_rate = 16.0
area = float(WIN * WIN)

VMEM = pltpu.VMEM
BF16 = jnp.bfloat16
F32 = jnp.float32


def tables():
    freq = np.arange(MODES) - MODES // 2
    angle = (2.0 * math.pi / WIN) * np.mod(freq[:, None] * np.arange(WIN)[None], WIN)
    cos, sin = np.cos(angle), np.sin(angle)
    stacked = np.concatenate([cos, sin], 0)
    forward = stacked.T
    core = slice(MARGIN, MARGIN + TILE)
    c_core, s_core = cos[:, core], sin[:, core]
    c_low, s_low = cos[:, ::STEP], sin[:, ::STEP]
    reach = HALF + MARGIN
    place_a = np.zeros((TILE, 2 * MODES))
    place_a[TILE - reach :] = forward[:reach]
    place_b = np.zeros((TILE, 2 * MODES))
    place_b[:reach] = forward[reach:]
    offset = np.arange(MARGIN, MARGIN + TILE)[:, None] - STEP * np.arange(COARSE)[None]
    orders = np.arange(1, 2 * MODES // 2)
    interp = 1.0 + 2.0 * np.cos((2.0 * math.pi / WIN) * orders[:, None, None] * offset[None]).sum(0)
    interp = (interp + np.cos((2.0 * math.pi / WIN) * MODES * offset)) / COARSE
    high = interp.astype(jnp.bfloat16).astype(np.float64)
    pad = np.zeros((COARSE, COARSE))
    table = dict(
        own=(forward[core], np.concatenate([c_core.T, -s_core.T], 1)),
        rim=(
            np.concatenate([forward[MARGIN + TILE :], forward[:MARGIN]], 0),
            np.concatenate([stacked[:, :MARGIN], stacked[:, MARGIN + TILE :]], 1),
        ),
        q_own=(stacked[:, core],),
        spread=(np.block([[c_low, s_low], [-s_low, c_low]]),),
        q_low=(np.concatenate([c_low.T, s_low.T], 1), pad),
        interp=(high, interp - high),
        interp_t=(np.concatenate([high.T, (interp - high).T], 0),),
        gather=(
            np.block(
                [[c_low.T, -s_low.T, -s_low.T, -c_low.T], [s_low.T, c_low.T, c_low.T, -s_low.T]]
            ),
        ),
        q_back=(c_low, s_low),
        inv_left=(np.block([[c_core[:, HALF:], s_core[:, HALF:]], [-s_core[:, HALF:], c_core[:, HALF:]]]),),
        inv_right=(np.block([[c_core[:, :HALF], s_core[:, :HALF]], [-s_core[:, :HALF], c_core[:, :HALF]]]),),
        place=(place_a, place_b),
        q_place=(np.concatenate([place_a.T, place_b.T], 0),),
    )
    table = {name: np.concatenate(value, 1) for name, value in table.items()}
    starts = dict(zip(table, np.cumsum([0] + [len(value) for value in table.values()])))
    rows = {name: slice(int(starts[name]), int(starts[name]) + len(table[name])) for name in table}
    return np.concatenate(list(table.values()), 0).astype(jnp.bfloat16), rows


TABLE, TABLE_ROWS = tables()


class Tables:
    def __init__(self, ref):
        self.ref = ref

    def __getitem__(self, name):
        return self.ref[TABLE_ROWS[name], :]

    def left(self, name):
        return self.ref[TABLE_ROWS[name], :COARSE]

    def right(self, name):
        return self.ref[TABLE_ROWS[name], COARSE:]


def dot(left, right):
    return jnp.dot(left, right, preferred_element_type=F32)


def swap_halves(value):
    return pltpu.roll(value, MODES, axis=1)


def low_lanes(shape):
    return lax.broadcasted_iota(jnp.int32, shape, 1) < MODES


def modes_of(blocks):
    top, bottom = blocks[:MODES], swap_halves(blocks[MODES:])
    return jnp.where(low_lanes(top.shape), top - bottom, -(top + bottom)) / area


def imaging_modes(spec, goal, weight, modes_ref, weight_ref, field_ref, grad_ref, t):
    swapped = swap_halves(spec)
    low = low_lanes(spec.shape)
    spec_a = jnp.where(low, spec, swapped)
    spec_b = jnp.where(low, -swapped, spec)
    filtered = []
    for k in range(KERN):
        resp = modes_ref[k]
        filtered.append((resp * spec_a + swap_halves(resp) * spec_b).astype(BF16))
    partial = dot(jnp.concatenate(filtered, 0), t["spread"]).astype(BF16)
    level = jnp.zeros((COARSE, COARSE), F32)
    for k in range(KERN):
        part = partial[k * MODES : (k + 1) * MODES]
        real, imag = part[:, :COARSE], part[:, COARSE:]
        rotated = jnp.concatenate([part, jnp.concatenate([-imag, real], 1)], 0)
        field = dot(t.left("q_low"), rotated)
        field_ref[k] = field
        a_real, a_imag = field[:, :COARSE], field[:, COARSE:]
        level = level + weight_ref[k] * (a_real * a_real + a_imag * a_imag)
    level = level.astype(BF16)
    half = dot(t["interp"], jnp.concatenate([level, level], 0)).astype(BF16)
    core = dot(jnp.concatenate([half, half], 1), t["interp_t"])
    printed = jax.nn.sigmoid(steepness * (core - threshold))
    core_grad = 2.0 * (printed - goal.astype(F32)) * printed * (1.0 - printed) * steepness
    if weight is not None:
        core_grad = jnp.where(weight, core_grad, 0.0)
    low_grad = dot(t["interp_t"][:COARSE], core_grad.astype(BF16)).astype(BF16)
    low_grad = dot(low_grad, t.left("interp"))
    both = jnp.concatenate([low_grad, low_grad], 1)
    for k in range(KERN):
        scaled = field_ref[k] * both * (2.0 * weight_ref[k])
        grad_ref[k * COARSE : (k + 1) * COARSE, :] = scaled.astype(BF16)
    gathered = dot(grad_ref[...], t["gather"]).astype(BF16)
    direct = jnp.zeros((MODES, 2 * MODES), F32)
    crossed = jnp.zeros((MODES, 2 * MODES), F32)
    for k in range(KERN):
        rows = gathered[k * COARSE : (k + 1) * COARSE]
        back = dot(t["q_back"], jnp.concatenate([rows[:, :COARSE], rows[:, COARSE:]], 0))
        resp = modes_ref[k]
        direct = direct + resp * back
        crossed = crossed + swap_halves(resp) * back
    return jnp.where(low, direct + swap_halves(direct), crossed - swap_halves(crossed)).astype(BF16)


def edges_kernel(mask_ref, target_ref, edges_ref, left_ref):
    wire = jax.nn.sigmoid(mask_ref[...])
    edges = jnp.concatenate([wire[:, :MARGIN], wire[:, TILE - MARGIN :]], 1).astype(BF16)
    edges_ref[...] = edges
    left_ref[:, : 2 * MARGIN] = edges
    left_ref[:, 2 * MARGIN :] = target_ref[:, :HALF]


def strip_kernel(
    cols, mask_ref, target_ref, left_ref, right_ref, table_ref, u_ref, even_ref, odd_ref
):
    t = Tables(table_ref)
    col = lax.axis_index("col")
    odd = lax.rem(lax.axis_index("row"), 2) == 1
    wire = jax.nn.sigmoid(mask_ref[...]).astype(BF16)
    low = low_lanes((TILE, 2 * MARGIN))
    keep = jnp.logical_or(
        jnp.logical_and(low, col < cols - 1), jnp.logical_and(jnp.logical_not(low), col > 0)
    )
    rim = jnp.where(low, right_ref[:, : 2 * MARGIN].astype(F32), left_ref[...].astype(F32))
    rim = jnp.where(keep, rim, 0.0).astype(BF16)
    half_spec = (dot(wire, t.left("own")) + dot(rim, t.left("rim"))).astype(BF16)
    u_ref[...] = half_spec
    goals = jnp.concatenate([target_ref[:HALF, HALF:], right_ref[:HALF, 2 * MARGIN :]], 0)
    top, bottom = half_spec[:MARGIN], half_spec[TILE - MARGIN :]

    @pl.when(odd)
    def _():
        even_ref[:MARGIN, :] = top
        odd_ref[:MARGIN, :] = bottom

    @pl.when(jnp.logical_not(odd))
    def _():
        even_ref[:MARGIN, :] = bottom
        odd_ref[:MARGIN, :] = top

    even_ref[MARGIN:, :] = goals
    odd_ref[MARGIN:, :] = goals


def first_kernel(
    rows, mask_ref, u_ref, even_ref, odd_ref, goal_ref, modes_ref, weight_ref, table_ref,
    first_ref, aa_ref, ab_ref, ba_ref, bb_ref, field_ref, grad_ref,
):
    t = Tables(table_ref)
    row = lax.axis_index("row")
    odd = lax.rem(row, 2) == 1
    even_in, odd_in = even_ref[:MARGIN, :].astype(F32), odd_ref[:MARGIN, :].astype(F32)
    above = jnp.where(row > 0, jnp.where(odd, even_in, odd_in), 0.0)
    below = jnp.where(row < rows - 1, jnp.where(odd, odd_in, even_in), 0.0)
    rim = jnp.concatenate([above, below], 0).astype(BF16)
    spec = modes_of(dot(t["q_own"], u_ref[...]) + dot(t.right("rim"), rim))
    combined = imaging_modes(
        spec, goal_ref[...], None, modes_ref, weight_ref, field_ref, grad_ref, t
    )
    left = dot(combined, t["inv_right"]).astype(BF16)
    right = dot(combined, t["inv_left"]).astype(BF16)
    real = jnp.concatenate([left[:, :HALF], right[:, :HALF]], 1)
    imag = jnp.concatenate([left[:, HALF:], right[:, HALF:]], 1)
    mask_grad = dot(t.right("own"), jnp.concatenate([real, imag], 0)) / area
    mask = mask_ref[...]
    soft = jax.nn.sigmoid(mask)
    first = mask - step_rate * (mask_grad * soft * (1.0 - soft))
    first_ref[...] = first
    wire = jax.nn.sigmoid(first).astype(BF16)
    half = dot(wire, t["place"])
    half_hi = half.astype(BF16)
    half_lo = (half - half_hi.astype(F32)).astype(BF16)
    blocks = dot(t["q_place"], half_hi) + dot(t["q_place"], half_lo)
    aa_ref[...] = modes_of(blocks[:HALF, :HALF])
    ab_ref[...] = modes_of(blocks[:HALF, HALF:])
    ba_ref[...] = modes_of(blocks[HALF:, :HALF])
    bb_ref[...] = modes_of(blocks[HALF:, HALF:])


def heal_kernel(
    rows, cols, own_ref, right_ref, below_ref, corner_ref, goal_ref, goal_right_ref, even_ref,
    odd_ref, modes_ref, weight_ref, table_ref, out_ref, field_ref, grad_ref,
):
    row = lax.axis_index("row")
    inner_row = row < rows - 1
    inner_col = lax.axis_index("col") < cols - 1
    spec = own_ref[...]
    spec = spec + jnp.where(inner_col, right_ref[...], 0.0)
    spec = spec + jnp.where(inner_row, below_ref[...], 0.0)
    spec = spec + jnp.where(jnp.logical_and(inner_row, inner_col), corner_ref[...], 0.0)
    upper = jnp.concatenate([goal_ref[HALF:, HALF:], goal_right_ref[HALF:, HALF:]], 1)
    lower = jnp.where(
        lax.rem(row, 2) == 1, odd_ref[MARGIN:, :].astype(F32), even_ref[MARGIN:, :].astype(F32)
    )
    lower = jnp.concatenate([lower[:HALF], lower[HALF:]], 1)
    goal = jnp.concatenate([upper.astype(F32), lower], 0)
    shape = (TILE, TILE)
    weight = jnp.logical_and(
        jnp.logical_or(lax.broadcasted_iota(jnp.int32, shape, 0) < HALF, inner_row),
        jnp.logical_or(lax.broadcasted_iota(jnp.int32, shape, 1) < HALF, inner_col),
    )
    out_ref[...] = imaging_modes(
        spec, goal, weight, modes_ref, weight_ref, field_ref, grad_ref, Tables(table_ref)
    )


def final_kernel(first_ref, own_ref, left_ref, up_ref, corner_ref, table_ref, out_ref):
    t = Tables(table_ref)
    has_row = lax.axis_index("row") > 0
    has_col = lax.axis_index("col") > 0

    def kept(ref, flag):
        return jnp.where(flag, ref[...].astype(F32), 0.0).astype(BF16)

    left = jnp.concatenate(
        [kept(left_ref, has_col), kept(corner_ref, jnp.logical_and(has_row, has_col))], 0
    )
    right = jnp.concatenate([own_ref[...], kept(up_ref, has_row)], 0)
    left = dot(left, t["inv_left"]).astype(BF16)
    right = dot(right, t["inv_right"]).astype(BF16)

    def quarter(rows):
        real = jnp.concatenate([left[rows, :HALF], right[rows, :HALF]], 1)
        imag = jnp.concatenate([left[rows, HALF:], right[rows, HALF:]], 1)
        return jnp.concatenate([real, imag], 0)

    q_inv = t.right("own")
    lower = dot(q_inv[:HALF], quarter(slice(0, MODES)))
    upper = dot(q_inv[HALF:], quarter(slice(MODES, 2 * MODES)))
    grad = jnp.concatenate([upper, lower], 0) / area
    first = first_ref[...]
    soft = jax.nn.sigmoid(first)
    out_ref[...] = first - step_rate * (grad * soft * (1.0 - soft))


VMEM_SPEC = pl.BlockSpec(memory_space=VMEM)
SMEM_SPEC = pl.BlockSpec(memory_space=pltpu.SMEM)
FIELD_SCRATCH = [VMEM((KERN, COARSE, 2 * COARSE), F32), VMEM((KERN * COARSE, 2 * COARSE), BF16)]


def shape_of(rows, cols, dtype):
    return jax.ShapeDtypeStruct((rows, cols), dtype)


def per_device(rows, cols, mask_param, target, kernel_modes, kernel_weight):
    table = jnp.asarray(TABLE)

    def permuted(value, place):
        pairs = [
            (r * cols + c, place(r, c)[0] * cols + place(r, c)[1])
            for r in range(rows)
            for c in range(cols)
        ]
        return lax.ppermute(value, ("row", "col"), pairs)

    def move(value, down, right):
        return permuted(value, lambda r, c: ((r + down) % rows, (c + right) % cols))

    def swap(value, parity):
        def place(r, c):
            other = r + 1 if r % 2 == parity else r - 1
            return (other, c) if 0 <= other < rows else (r, c ^ 1)

        return permuted(value, place)

    def call(kernel, outs, smem, limit, scratch, name, *args):
        specs = [SMEM_SPEC if i in smem else VMEM_SPEC for i in range(len(args))]
        return pl.pallas_call(
            kernel, out_shape=outs, in_specs=specs,
            out_specs=jax.tree.map(lambda _: VMEM_SPEC, outs), scratch_shapes=scratch,
            compiler_params=pltpu.CompilerParams(vmem_limit_bytes=limit << 20), name=name,
        )(*args)

    edges, edges_left = call(
        edges_kernel, (shape_of(TILE, 2 * MARGIN, BF16), shape_of(TILE, TILE, BF16)),
        (), 4, (), "edges", mask_param, target,
    )
    from_left = move(edges, 0, 1)
    from_right = move(edges_left, 0, -1)
    rim_shape = shape_of(MARGIN + TILE, 2 * MODES, BF16)
    half_spec, even_rim, odd_rim = call(
        lambda *refs: strip_kernel(cols, *refs),
        (shape_of(TILE, 2 * MODES, BF16), rim_shape, rim_shape), (), 4, (), "strip",
        mask_param, target, from_left, from_right, table,
    )
    even_rim, odd_rim = swap(even_rim, 0), swap(odd_rim, 1)
    modes_shape = shape_of(MODES, 2 * MODES, F32)
    first, own, to_left, to_up, to_corner = call(
        lambda *refs: first_kernel(rows, *refs),
        (shape_of(TILE, TILE, F32),) + (modes_shape,) * 4, (6,), 12, FIELD_SCRATCH, "first",
        mask_param, half_spec, even_rim, odd_rim, target, kernel_modes, kernel_weight, table,
    )
    spec_right = move(to_left, 0, -1)
    spec_below = move(to_up, -1, 0)
    spec_corner = move(to_corner, -1, -1)
    combined = call(
        lambda *refs: heal_kernel(rows, cols, *refs),
        shape_of(MODES, 2 * MODES, BF16), (9,), 12, FIELD_SCRATCH, "heal",
        own, spec_right, spec_below, spec_corner, target, from_right, even_rim, odd_rim,
        kernel_modes, kernel_weight, table,
    )
    mode_left = move(combined, 0, 1)
    mode_up = move(combined, 1, 0)
    mode_corner = move(combined, 1, 1)
    return call(
        final_kernel, shape_of(TILE, TILE, F32), (), 4, (), "final",
        first, combined, mode_left, mode_up, mode_corner, table,
    )


def solution(mesh):
    rows, cols = mesh.shape["row"], mesh.shape["col"]
    tile = P(("grp", "row"), "col")
    return jax.shard_map(
        lambda *args: per_device(rows, cols, *args), mesh=mesh,
        in_specs=(tile, tile, P(), P()), out_specs=tile, check_vma=False,
    )
```

```python
import math

import jax
import jax.numpy as jnp
import numpy as np
from jax import lax
from jax.experimental import pallas as pl
from jax.experimental.pallas import tpu as pltpu
from jax.sharding import PartitionSpec as P

TILE = 256
MARGIN = 64
MODES = 64
KERN = 12
HALF = 128
WIN = 384
COARSE = 128
STEP = WIN // COARSE

steepness = 4.0
threshold = 0.4
step_rate = 16.0
area = float(WIN * WIN)

VMEM = pltpu.VMEM
BF16 = jnp.bfloat16
F32 = jnp.float32


def tables():
    freq = np.arange(MODES) - MODES // 2
    angle = (2.0 * math.pi / WIN) * np.mod(freq[:, None] * np.arange(WIN)[None], WIN)
    cos, sin = np.cos(angle), np.sin(angle)
    stacked = np.concatenate([cos, sin], 0)
    forward = stacked.T
    core = slice(MARGIN, MARGIN + TILE)
    c_core, s_core = cos[:, core], sin[:, core]
    c_low, s_low = cos[:, ::STEP], sin[:, ::STEP]
    reach = HALF + MARGIN
    place_a = np.zeros((TILE, 2 * MODES))
    place_a[TILE - reach :] = forward[:reach]
    place_b = np.zeros((TILE, 2 * MODES))
    place_b[:reach] = forward[reach:]
    offset = np.arange(MARGIN, MARGIN + TILE)[:, None] - STEP * np.arange(COARSE)[None]
    orders = np.arange(1, 2 * MODES // 2)
    interp = 1.0 + 2.0 * np.cos((2.0 * math.pi / WIN) * orders[:, None, None] * offset[None]).sum(0)
    interp = (interp + np.cos((2.0 * math.pi / WIN) * MODES * offset)) / COARSE
    high = interp.astype(jnp.bfloat16).astype(np.float64)
    pad = np.zeros((COARSE, COARSE))
    table = dict(
        own=(forward[core], np.concatenate([c_core.T, -s_core.T], 1)),
        rim=(
            np.concatenate([forward[MARGIN + TILE :], forward[:MARGIN]], 0),
            np.concatenate([stacked[:, :MARGIN], stacked[:, MARGIN + TILE :]], 1),
        ),
        q_own=(stacked[:, core],),
        spread=(np.block([[c_low, s_low], [-s_low, c_low]]),),
        q_low=(np.concatenate([c_low.T, s_low.T], 1), pad),
        interp=(high, interp - high),
        interp_t=(np.concatenate([high.T, (interp - high).T], 0),),
        gather=(
            np.block(
                [[c_low.T, -s_low.T, -s_low.T, -c_low.T], [s_low.T, c_low.T, c_low.T, -s_low.T]]
            ),
        ),
        q_back=(c_low, s_low),
        inv_left=(np.block([[c_core[:, HALF:], s_core[:, HALF:]], [-s_core[:, HALF:], c_core[:, HALF:]]]),),
        inv_right=(np.block([[c_core[:, :HALF], s_core[:, :HALF]], [-s_core[:, :HALF], c_core[:, :HALF]]]),),
        place=(place_a, place_b),
        q_place=(np.concatenate([place_a.T, place_b.T], 0),),
    )
    table = {name: np.concatenate(value, 1) for name, value in table.items()}
    arrays, rows = [], {}
    for names in (("own", "rim"), tuple(name for name in table if name not in ("own", "rim"))):
        start = 0
        for name in names:
            rows[name] = slice(start, start + len(table[name]))
            start = rows[name].stop
        arrays.append(np.concatenate([table[name] for name in names], 0).astype(jnp.bfloat16))
    return arrays, rows


(EDGE_TABLE, MAIN_TABLE), TABLE_ROWS = tables()


class Tables:
    def __init__(self, ref):
        self.ref = ref

    def __getitem__(self, name):
        return self.ref[TABLE_ROWS[name], :]

    def left(self, name):
        return self.ref[TABLE_ROWS[name], :COARSE]

    def right(self, name):
        return self.ref[TABLE_ROWS[name], COARSE:]


def dot(left, right):
    return jnp.dot(left, right, preferred_element_type=F32)


def swap_halves(value):
    return pltpu.roll(value, MODES, axis=1)


def low_lanes(shape):
    return lax.broadcasted_iota(jnp.int32, shape, 1) < MODES


def modes_of(blocks):
    top, bottom = blocks[:MODES], swap_halves(blocks[MODES:])
    return jnp.where(low_lanes(top.shape), top - bottom, -(top + bottom)) / area


HALVES = (range(KERN // 2), range(KERN // 2, KERN))


def imaging_modes(spec, goal, inner, resp_ref, swapped_ref, scaled_ref, cross_ref, weight_ref, field_ref, t):
    swapped = swap_halves(spec)
    low = low_lanes(spec.shape)
    spec_a = jnp.where(low, spec, swapped)
    spec_b = jnp.where(low, -swapped, spec)
    partial = []
    for half in HALVES:
        filtered = [(resp_ref[k] * spec_a + swapped_ref[k] * spec_b).astype(BF16) for k in half]
        spread = dot(jnp.concatenate(filtered, 0), t["spread"]).astype(BF16)
        partial += [spread[i * MODES : (i + 1) * MODES] for i in range(len(half))]
    level = jnp.zeros((COARSE, COARSE), F32)
    for k, part in enumerate(partial):
        real, imag = part[:, :COARSE], part[:, COARSE:]
        rotated = jnp.concatenate([part, jnp.concatenate([-imag, real], 1)], 0)
        field = dot(t.left("q_low"), rotated)
        field_ref[k] = field
        a_real, a_imag = field[:, :COARSE], field[:, COARSE:]
        level = level + weight_ref[k] * (a_real * a_real + a_imag * a_imag)
    level = (2.0 * level - 2.0 * threshold).astype(BF16)
    half = dot(t["interp"], jnp.concatenate([level, level], 0)).astype(BF16)
    core = dot(jnp.concatenate([half, half], 1), t["interp_t"])
    rise = jnp.tanh(core)
    core_grad = ((rise + (1.0 - 2.0 * goal.astype(F32))) * (1.0 - rise * rise)).astype(BF16)
    rows_low, cols_low = t["interp_t"][:COARSE], t.left("interp")
    if inner is not None:
        inner_row, inner_col = inner
        outer = jnp.where(inner_row, rows_low[:, HALF:].astype(F32), 0.0).astype(BF16)
        rows_low = jnp.concatenate([rows_low[:, :HALF], outer], 1)
        outer = jnp.where(inner_col, cols_low[HALF:].astype(F32), 0.0).astype(BF16)
        cols_low = jnp.concatenate([cols_low[:HALF], outer], 0)
    low_grad = dot(dot(rows_low, core_grad).astype(BF16), cols_low)
    both = jnp.concatenate([low_grad, low_grad], 1)
    gathered = []
    for half in HALVES:
        shaded = jnp.concatenate([(field_ref[k] * both).astype(BF16) for k in half], 0)
        rows = dot(shaded, t["gather"]).astype(BF16)
        gathered += [rows[i * COARSE : (i + 1) * COARSE] for i in range(len(half))]
    direct = jnp.zeros((MODES, 2 * MODES), F32)
    crossed = jnp.zeros((MODES, 2 * MODES), F32)
    for k, rows in enumerate(gathered):
        back = dot(t["q_back"], jnp.concatenate([rows[:, :COARSE], rows[:, COARSE:]], 0))
        direct = direct + scaled_ref[k] * back
        crossed = crossed + cross_ref[k] * back
    return jnp.where(low, direct + swap_halves(direct), crossed - swap_halves(crossed)).astype(BF16)


def edges_kernel(mask_ref, target_ref, left_ref, right_ref, mask_out_ref, target_out_ref):
    low = low_lanes((TILE, 2 * MARGIN))
    edge = jax.nn.sigmoid(jnp.where(low, mask_ref[:, : 2 * MARGIN], mask_ref[:, HALF:]))
    top, bottom = edge[:HALF], edge[HALF:]
    low = low[:HALF]
    left_ref[:HALF, :] = jnp.where(low, top, swap_halves(bottom)).astype(BF16)
    right_ref[...] = jnp.where(low, swap_halves(top), bottom).astype(BF16)
    left_ref[HALF:, :] = target_ref[:, :HALF]
    mask_out_ref[...] = mask_ref[...]
    target_out_ref[...] = target_ref[...]


def table_kernel(table_ref, after_ref, out_ref):
    out_ref[...] = table_ref[...]


def responses_kernel(modes_ref, weight_ref, after_ref, swapped_ref, scaled_ref, cross_ref):
    for k in range(KERN):
        resp = modes_ref[k]
        swapped = swap_halves(resp)
        swapped_ref[k] = swapped
        scaled_ref[k] = (2.0 * weight_ref[k]) * resp
        cross_ref[k] = (2.0 * weight_ref[k]) * swapped


def strip_kernel(
    cols, mask_ref, target_ref, left_ref, right_ref, table_ref, u_ref, even_ref, odd_ref
):
    t = Tables(table_ref)
    col = lax.axis_index("col")
    odd = lax.rem(lax.axis_index("row"), 2) == 1
    wire = jax.nn.sigmoid(mask_ref[...]).astype(BF16)
    low = low_lanes((HALF, 2 * MARGIN))
    right = jnp.where(col < cols - 1, right_ref[:HALF, :].astype(F32), 0.0)
    left = jnp.where(col > 0, left_ref[...].astype(F32), 0.0)
    rim = jnp.concatenate(
        [jnp.where(low, right, swap_halves(left)), jnp.where(low, swap_halves(right), left)], 0
    ).astype(BF16)
    half_spec = (dot(wire, t.left("own")) + dot(rim, t.left("rim"))).astype(BF16)
    u_ref[...] = half_spec
    top, bottom = half_spec[:MARGIN], half_spec[TILE - MARGIN :]

    @pl.when(odd)
    def _():
        even_ref[:MARGIN, :] = top
        odd_ref[:MARGIN, :] = bottom

    @pl.when(jnp.logical_not(odd))
    def _():
        even_ref[:MARGIN, :] = bottom
        odd_ref[:MARGIN, :] = top

    for ref in (even_ref, odd_ref):
        ref[MARGIN : MARGIN + HALF, :] = target_ref[:HALF, HALF:]
        ref[MARGIN + HALF :, :] = right_ref[HALF : 2 * HALF, :]


def first_kernel(
    rows, mask_ref, u_ref, even_ref, odd_ref, goal_ref, resp_ref, swapped_ref, scaled_ref,
    cross_ref, weight_ref, edge_table_ref, table_ref, first_ref, aa_ref, ab_ref, ba_ref, bb_ref,
    field_ref,
):
    edge, t = Tables(edge_table_ref), Tables(table_ref)
    row = lax.axis_index("row")
    odd = lax.rem(row, 2) == 1
    even_in, odd_in = even_ref[:MARGIN, :].astype(F32), odd_ref[:MARGIN, :].astype(F32)
    above = jnp.where(row > 0, jnp.where(odd, even_in, odd_in), 0.0)
    below = jnp.where(row < rows - 1, jnp.where(odd, odd_in, even_in), 0.0)
    rim = jnp.concatenate([above, below], 0).astype(BF16)
    spec = modes_of(dot(t["q_own"], u_ref[...]) + dot(edge.right("rim"), rim))
    combined = imaging_modes(
        spec, goal_ref[...], None, resp_ref, swapped_ref, scaled_ref, cross_ref, weight_ref,
        field_ref, t,
    )
    left = dot(combined, t["inv_right"]).astype(BF16)
    right = dot(combined, t["inv_left"]).astype(BF16)
    real = jnp.concatenate([left[:, :HALF], right[:, :HALF]], 1)
    imag = jnp.concatenate([left[:, HALF:], right[:, HALF:]], 1)
    mask_grad = dot(edge.right("own"), jnp.concatenate([real, imag], 0))
    mask = mask_ref[...]
    first = updated(mask, mask_grad)
    first_ref[...] = first
    half = dot(jax.nn.sigmoid(first).astype(BF16), t["place"])
    half_hi = half.astype(BF16)
    half_lo = (half - half_hi.astype(F32)).astype(BF16)
    blocks = dot(t["q_place"], half_hi) + dot(t["q_place"], half_lo)
    aa_ref[...] = modes_of(blocks[:HALF, :HALF])
    ab_ref[...] = modes_of(blocks[:HALF, HALF:])
    ba_ref[...] = modes_of(blocks[HALF:, :HALF])
    bb_ref[...] = modes_of(blocks[HALF:, HALF:])


def updated(param, grad):
    rise = jnp.tanh(0.5 * param)
    return param - (step_rate / 4.0 / area) * (grad * (1.0 - rise * rise))


def heal_kernel(
    rows, cols, own_ref, right_ref, below_ref, corner_ref, goal_ref, goal_right_ref, even_ref,
    odd_ref, resp_ref, swapped_ref, scaled_ref, cross_ref, weight_ref, table_ref, out_ref, field_ref,
):
    row = lax.axis_index("row")
    inner_row = row < rows - 1
    inner_col = lax.axis_index("col") < cols - 1
    spec = own_ref[...]
    spec = spec + jnp.where(inner_col, right_ref[...], 0.0)
    spec = spec + jnp.where(inner_row, below_ref[...], 0.0)
    spec = spec + jnp.where(jnp.logical_and(inner_row, inner_col), corner_ref[...], 0.0)
    upper = jnp.concatenate([goal_ref[HALF:, HALF:], goal_right_ref[2 * HALF :, :]], 1)
    lower = jnp.where(
        lax.rem(row, 2) == 1, odd_ref[MARGIN:, :].astype(F32), even_ref[MARGIN:, :].astype(F32)
    )
    lower = jnp.concatenate([lower[:HALF], lower[HALF:]], 1)
    goal = jnp.concatenate([upper.astype(F32), lower], 0)
    out_ref[...] = imaging_modes(
        spec, goal, (inner_row, inner_col), resp_ref, swapped_ref, scaled_ref, cross_ref,
        weight_ref, field_ref, Tables(table_ref),
    )


def final_kernel(
    first_ref, own_ref, left_ref, up_ref, corner_ref, edge_table_ref, table_ref, out_ref
):
    edge, t = Tables(edge_table_ref), Tables(table_ref)
    has_row = lax.axis_index("row") > 0
    has_col = lax.axis_index("col") > 0

    def kept(ref, flag):
        return jnp.where(flag, ref[...].astype(F32), 0.0).astype(BF16)

    left = jnp.concatenate(
        [kept(left_ref, has_col), kept(corner_ref, jnp.logical_and(has_row, has_col))], 0
    )
    right = jnp.concatenate([own_ref[...], kept(up_ref, has_row)], 0)
    left = dot(left, t["inv_left"]).astype(BF16)
    right = dot(right, t["inv_right"]).astype(BF16)

    def quarter(rows):
        real = jnp.concatenate([left[rows, :HALF], right[rows, :HALF]], 1)
        imag = jnp.concatenate([left[rows, HALF:], right[rows, HALF:]], 1)
        return jnp.concatenate([real, imag], 0)

    q_inv = edge.right("own")
    lower = dot(q_inv[:HALF], quarter(slice(0, MODES)))
    upper = dot(q_inv[HALF:], quarter(slice(MODES, 2 * MODES)))
    out_ref[:HALF, :] = updated(first_ref[:HALF, :], upper)
    out_ref[HALF:, :] = updated(first_ref[HALF:, :], lower)


VMEM_SPEC = pl.BlockSpec(memory_space=VMEM)
SMEM_SPEC = pl.BlockSpec(memory_space=pltpu.SMEM)
FIELD_SCRATCH = [VMEM((KERN, COARSE, 2 * COARSE), F32)]


def shape_of(rows, cols, dtype):
    return jax.ShapeDtypeStruct((rows, cols), dtype)


def per_device(rows, cols, mask_param, target, kernel_modes, kernel_weight):
    table, edge_table = jnp.asarray(MAIN_TABLE), jnp.asarray(EDGE_TABLE)

    def permuted(value, place):
        pairs = [
            (r * cols + c, place(r, c)[0] * cols + place(r, c)[1])
            for r in range(rows)
            for c in range(cols)
        ]
        return lax.ppermute(value, ("row", "col"), pairs)

    def move(value, down, right):
        return permuted(value, lambda r, c: ((r + down) % rows, (c + right) % cols))

    def swap(value, parity):
        def place(r, c):
            other = r + 1 if r % 2 == parity else r - 1
            return (other, c) if 0 <= other < rows else (r, c ^ 1)

        return permuted(value, place)

    def call(kernel, outs, other, limit, scratch, name, *args):
        return pl.pallas_call(
            kernel, out_shape=outs, in_specs=[other.get(i, VMEM_SPEC) for i in range(len(args))],
            out_specs=jax.tree.map(lambda _: VMEM_SPEC, outs), scratch_shapes=scratch,
            compiler_params=pltpu.CompilerParams(
                vmem_limit_bytes=limit
            ),
            name=name,
        )(*args)

    to_left, to_right, mask, goal = call(
        edges_kernel,
        (
            shape_of(HALF + TILE, HALF, BF16), shape_of(HALF, HALF, BF16),
            shape_of(TILE, TILE, F32), shape_of(TILE, TILE, BF16),
        ),
        {}, 4 << 20, (), "edges", mask_param, target,
    )
    edge_table = call(
        table_kernel, shape_of(*EDGE_TABLE.shape, BF16), {}, 4 << 20, (), "table",
        edge_table, to_right,
    )
    from_right = move(to_left, 0, -1)
    from_left = move(to_right, 0, 1)
    resp_shape = jax.ShapeDtypeStruct(kernel_modes.shape, F32)
    responses = call(
        responses_kernel, (resp_shape,) * 3, {1: SMEM_SPEC}, 4 << 20, (), "responses",
        kernel_modes, kernel_weight, to_right,
    )
    rim_shape = shape_of(MARGIN + TILE, 2 * MODES, BF16)
    half_spec, even_rim, odd_rim = call(
        lambda *refs: strip_kernel(cols, *refs),
        (shape_of(TILE, 2 * MODES, BF16), rim_shape, rim_shape), {}, 4 << 20, (), "strip",
        mask, goal, from_left, from_right, edge_table,
    )
    even_rim, odd_rim = swap(even_rim, 0), swap(odd_rim, 1)
    modes_shape = shape_of(MODES, 2 * MODES, F32)
    first, own, to_left, to_up, to_corner = call(
        lambda *refs: first_kernel(rows, *refs),
        (shape_of(TILE, TILE, F32),) + (modes_shape,) * 4, {9: SMEM_SPEC}, 12 << 20, FIELD_SCRATCH,
        "first", mask, half_spec, even_rim, odd_rim, goal, kernel_modes, *responses,
        kernel_weight, edge_table, table,
    )
    spec_corner = move(to_corner, -1, -1)
    spec_below = move(to_up, -1, 0)
    spec_right = move(to_left, 0, -1)
    combined = call(
        lambda *refs: heal_kernel(rows, cols, *refs),
        shape_of(MODES, 2 * MODES, BF16), {12: SMEM_SPEC}, 12 << 20, FIELD_SCRATCH, "heal",
        own, spec_right, spec_below, spec_corner, goal, from_right, even_rim, odd_rim,
        kernel_modes, *responses, kernel_weight, table,
    )
    mode_corner = move(combined, 1, 1)
    mode_up = move(combined, 1, 0)
    mode_left = move(combined, 0, 1)
    return call(
        final_kernel, shape_of(TILE, TILE, F32), {}, 4 << 20, (), "final",
        first, combined, mode_left, mode_up, mode_corner, edge_table, table,
    )


def solution(mesh):
    rows, cols = mesh.shape["row"], mesh.shape["col"]
    tile = P(("grp", "row"), "col")
    return jax.shard_map(
        lambda *args: per_device(rows, cols, *args), mesh=mesh,
        in_specs=(tile, tile, P(), P()), out_specs=tile, check_vma=False,
    )
```

```python
import math

import jax
import jax.numpy as jnp
import numpy as np
from jax import lax
from jax.experimental import pallas as pl
from jax.experimental.pallas import tpu as pltpu
from jax.sharding import PartitionSpec as P

TILE = 256
MARGIN = 64
MODES = 64
KERN = 12
HALF = 128
WIN = 384
COARSE = 128
STEP = WIN // COARSE

steepness = 4.0
threshold = 0.4
step_rate = 16.0
area = float(WIN * WIN)

VMEM = pltpu.VMEM
BF16 = jnp.bfloat16
F32 = jnp.float32


def tables():
    freq = np.arange(MODES) - MODES // 2
    angle = (2.0 * math.pi / WIN) * np.mod(freq[:, None] * np.arange(WIN)[None], WIN)
    cos, sin = np.cos(angle), np.sin(angle)
    stacked = np.concatenate([cos, sin], 0)
    forward = stacked.T
    core = slice(MARGIN, MARGIN + TILE)
    c_core, s_core = cos[:, core], sin[:, core]
    c_low, s_low = cos[:, ::STEP], sin[:, ::STEP]
    reach = HALF + MARGIN
    place_a = np.zeros((TILE, 2 * MODES))
    place_a[TILE - reach :] = forward[:reach]
    place_b = np.zeros((TILE, 2 * MODES))
    place_b[:reach] = forward[reach:]
    offset = np.arange(MARGIN, MARGIN + TILE)[:, None] - STEP * np.arange(COARSE)[None]
    orders = np.arange(1, 2 * MODES // 2)
    interp = 1.0 + 2.0 * np.cos((2.0 * math.pi / WIN) * orders[:, None, None] * offset[None]).sum(0)
    interp = (interp + np.cos((2.0 * math.pi / WIN) * MODES * offset)) / COARSE
    high = interp.astype(jnp.bfloat16).astype(np.float64)
    pad = np.zeros((COARSE, COARSE))
    table = dict(
        own=(forward[core], np.concatenate([c_core.T, -s_core.T], 1)),
        rim=(
            np.concatenate([forward[MARGIN + TILE :], forward[:MARGIN]], 0),
            np.concatenate([stacked[:, :MARGIN], stacked[:, MARGIN + TILE :]], 1),
        ),
        q_own=(stacked[:, core],),
        spread=(np.block([[c_low, s_low], [-s_low, c_low]]),),
        q_low=(np.concatenate([c_low.T, s_low.T], 1), pad),
        interp=(high, interp - high),
        interp_t=(np.concatenate([high.T, (interp - high).T], 0),),
        gather=(
            np.block(
                [[c_low.T, -s_low.T, -s_low.T, -c_low.T], [s_low.T, c_low.T, c_low.T, -s_low.T]]
            ),
        ),
        q_back=(c_low, s_low),
        inv_left=(np.block([[c_core[:, HALF:], s_core[:, HALF:]], [-s_core[:, HALF:], c_core[:, HALF:]]]),),
        inv_right=(np.block([[c_core[:, :HALF], s_core[:, :HALF]], [-s_core[:, :HALF], c_core[:, :HALF]]]),),
        place=(place_a, place_b),
        q_place=(np.concatenate([place_a.T, place_b.T], 0),),
    )
    table = {name: np.concatenate(value, 1) for name, value in table.items()}
    arrays, rows = [], {}
    for names in (("own", "rim"), tuple(name for name in table if name not in ("own", "rim"))):
        start = 0
        for name in names:
            rows[name] = slice(start, start + len(table[name]))
            start = rows[name].stop
        arrays.append(np.concatenate([table[name] for name in names], 0).astype(jnp.bfloat16))
    return arrays, rows


(EDGE_TABLE, MAIN_TABLE), TABLE_ROWS = tables()


class Tables:
    def __init__(self, ref):
        self.ref = ref

    def __getitem__(self, name):
        return self.ref[TABLE_ROWS[name], :]

    def left(self, name):
        return self.ref[TABLE_ROWS[name], :COARSE]

    def right(self, name):
        return self.ref[TABLE_ROWS[name], COARSE:]


def dot(left, right):
    return jnp.dot(left, right, preferred_element_type=F32)


def swap_halves(value):
    return pltpu.roll(value, MODES, axis=1)


def low_lanes(shape):
    return lax.broadcasted_iota(jnp.int32, shape, 1) < MODES


def modes_of(blocks):
    top, bottom = blocks[:MODES], swap_halves(blocks[MODES:])
    return jnp.where(low_lanes(top.shape), top - bottom, -(top + bottom)) / area


def imaging_modes(windows, resp_ref, swapped_ref, scaled_ref, cross_ref, weight_ref, field_ref, t):
    count = len(windows)
    low = low_lanes((MODES, 2 * MODES))
    cuts = 2 if count == 1 else 1
    groups = [range(i * KERN // cuts, (i + 1) * KERN // cuts) for i in range(cuts)]
    partials = []
    for spec, _, _ in windows:
        swapped = swap_halves(spec)
        spec_a = jnp.where(low, spec, swapped)
        spec_b = jnp.where(low, -swapped, spec)
        partial = []
        for group in groups:
            filtered = [(resp_ref[k] * spec_a + swapped_ref[k] * spec_b).astype(BF16) for k in group]
            spread = dot(jnp.concatenate(filtered, 0), t["spread"]).astype(BF16)
            partial += [spread[i * MODES : (i + 1) * MODES] for i in range(len(group))]
        partials.append(partial)
    levels = []
    for w, partial in enumerate(partials):
        level = jnp.zeros((COARSE, COARSE), F32)
        for k, part in enumerate(partial):
            real, imag = part[:, :COARSE], part[:, COARSE:]
            rotated = jnp.concatenate([part, jnp.concatenate([-imag, real], 1)], 0)
            field = dot(t.left("q_low"), rotated)
            field_ref[w * KERN + k] = field
            a_real, a_imag = field[:, :COARSE], field[:, COARSE:]
            level = level + weight_ref[k : k + 1, :] * (a_real * a_real + a_imag * a_imag)
        levels.append((2.0 * level - 2.0 * threshold).astype(BF16))
    halves = [dot(t["interp"], jnp.concatenate([level, level], 0)).astype(BF16) for level in levels]
    cores = [dot(jnp.concatenate([half, half], 1), t["interp_t"]) for half in halves]
    lows = []
    for core, (_, goal, inner) in zip(cores, windows):
        rise = jnp.tanh(core)
        core_grad = ((rise + (1.0 - 2.0 * goal.astype(F32))) * (1.0 - rise * rise)).astype(BF16)
        rows_low, cols_low = t["interp_t"][:COARSE], t.left("interp")
        inner_row, inner_col = inner
        if inner_row is not None:
            outer = jnp.where(inner_row, rows_low[:, HALF:].astype(F32), 0.0).astype(BF16)
            rows_low = jnp.concatenate([rows_low[:, :HALF], outer], 1)
        if inner_col is not None:
            outer = jnp.where(inner_col, cols_low[HALF:].astype(F32), 0.0).astype(BF16)
            cols_low = jnp.concatenate([cols_low[:HALF], outer], 0)
        lows.append((dot(rows_low, core_grad).astype(BF16), cols_low))
    lows = [dot(left, right) for left, right in lows]
    gathers = []
    for w, low_grad in enumerate(lows):
        both = jnp.concatenate([low_grad, low_grad], 1)
        gathered = []
        for group in groups:
            shaded = [(field_ref[w * KERN + k] * both).astype(BF16) for k in group]
            rows = dot(jnp.concatenate(shaded, 0), t["gather"]).astype(BF16)
            gathered += [rows[i * COARSE : (i + 1) * COARSE] for i in range(len(group))]
        gathers.append(gathered)
    results = []
    for gathered in gathers:
        direct = jnp.zeros((MODES, 2 * MODES), F32)
        crossed = jnp.zeros((MODES, 2 * MODES), F32)
        for k in range(0, KERN, 2):
            one, two = gathered[k], gathered[k + 1]
            upper = jnp.concatenate([one[:, :COARSE], two[:, :COARSE]], 1)
            lower = jnp.concatenate([one[:, COARSE:], two[:, COARSE:]], 1)
            back = dot(t["q_back"], jnp.concatenate([upper, lower], 0))
            for i, part in enumerate((back[:, : 2 * MODES], back[:, 2 * MODES :])):
                direct = direct + scaled_ref[k + i] * part
                crossed = crossed + cross_ref[k + i] * part
        results.append(
            jnp.where(low, direct + swap_halves(direct), crossed - swap_halves(crossed)).astype(BF16)
        )
    return results


def edges_kernel(mask_ref, target_ref, left_ref, right_ref, mask_out_ref, target_out_ref):
    low = low_lanes((TILE, 2 * MARGIN))
    edge = jax.nn.sigmoid(jnp.where(low, mask_ref[:, : 2 * MARGIN], mask_ref[:, HALF:]))
    top, bottom = edge[:HALF], edge[HALF:]
    low = low[:HALF]
    left_ref[:HALF, :] = jnp.where(low, top, swap_halves(bottom)).astype(BF16)
    right_ref[:HALF, :] = jnp.where(low, swap_halves(top), bottom).astype(BF16)
    left_ref[HALF:, :] = target_ref[:, :HALF]
    right_ref[HALF:, :] = target_ref[:, HALF:]
    mask_out_ref[...] = mask_ref[...]
    target_out_ref[...] = target_ref[...]


def table_kernel(table_ref, after_ref, out_ref):
    out_ref[...] = table_ref[...]


def responses_kernel(
    modes_ref, weight_ref, after_ref, swapped_ref, scaled_ref, cross_ref, weight_rows_ref
):
    for k in range(KERN):
        weight_rows_ref[k : k + 1, :] = jnp.full((1, COARSE), weight_ref[k], F32)
        resp = modes_ref[k]
        swapped = swap_halves(resp)
        swapped_ref[k] = swapped
        scaled_ref[k] = (2.0 * weight_ref[k]) * resp
        cross_ref[k] = (2.0 * weight_ref[k]) * swapped


def by_parity(odd, even_ref, odd_ref, below, above):
    @pl.when(odd)
    def _():
        even_ref[...] = above
        odd_ref[...] = below

    @pl.when(jnp.logical_not(odd))
    def _():
        even_ref[...] = below
        odd_ref[...] = above


def below_above(odd, even_ref, odd_ref):
    even, odd_value = even_ref[...].astype(F32), odd_ref[...].astype(F32)
    return jnp.where(odd, odd_value, even), jnp.where(odd, even, odd_value)


def strip_kernel(
    cols, mask_ref, target_ref, left_ref, right_ref, table_ref, u_ref, even_ref, odd_ref,
    even_goal_ref, odd_goal_ref,
):
    t = Tables(table_ref)
    col = lax.axis_index("col")
    odd = lax.rem(lax.axis_index("row"), 2) == 1
    wire = jax.nn.sigmoid(mask_ref[...]).astype(BF16)
    low = low_lanes((HALF, 2 * MARGIN))
    right = jnp.where(col < cols - 1, right_ref[:HALF, :].astype(F32), 0.0)
    left = jnp.where(col > 0, left_ref[:HALF, :].astype(F32), 0.0)
    rim = jnp.concatenate(
        [jnp.where(low, right, swap_halves(left)), jnp.where(low, swap_halves(right), left)], 0
    ).astype(BF16)
    half_spec = (dot(wire, t.left("own")) + dot(rim, t.left("rim"))).astype(BF16)
    u_ref[...] = half_spec
    by_parity(odd, even_ref, odd_ref, half_spec[TILE - MARGIN :], half_spec[:MARGIN])
    goals = jnp.concatenate([left_ref[HALF:, :], target_ref[...], right_ref[HALF:, :]], 1)
    by_parity(odd, even_goal_ref, odd_goal_ref, goals[HALF:], goals[:HALF])


def first_kernel(
    rows, mask_ref, u_ref, even_ref, odd_ref, goal_ref, resp_ref, swapped_ref, scaled_ref,
    cross_ref, weight_ref, edge_table_ref, table_ref, first_ref, left_ref, right_ref, field_ref,
):
    edge, t = Tables(edge_table_ref), Tables(table_ref)
    row = lax.axis_index("row")
    below, above = below_above(lax.rem(row, 2) == 1, even_ref, odd_ref)
    above = jnp.where(row > 0, above, 0.0)
    below = jnp.where(row < rows - 1, below, 0.0)
    rim = jnp.concatenate([above, below], 0).astype(BF16)
    spec = modes_of(dot(t["q_own"], u_ref[...]) + dot(edge.right("rim"), rim))
    (combined,) = imaging_modes(
        [(spec, goal_ref[...], (None, None))], resp_ref, swapped_ref, scaled_ref, cross_ref,
        weight_ref, field_ref, t,
    )
    left = dot(combined, t["inv_right"]).astype(BF16)
    right = dot(combined, t["inv_left"]).astype(BF16)
    real = jnp.concatenate([left[:, :HALF], right[:, :HALF]], 1)
    imag = jnp.concatenate([left[:, HALF:], right[:, HALF:]], 1)
    mask_grad = dot(edge.right("own"), jnp.concatenate([real, imag], 0))
    mask = mask_ref[...]
    first = updated(mask, mask_grad)
    first_ref[...] = first
    half = dot(jax.nn.sigmoid(first).astype(BF16), t["place"])
    half_hi = half.astype(BF16)
    half_lo = (half - half_hi.astype(F32)).astype(BF16)
    blocks = dot(t["q_place"], half_hi) + dot(t["q_place"], half_lo)
    right_ref[:MODES, :] = modes_of(blocks[:HALF, :HALF])
    left_ref[:MODES, :] = modes_of(blocks[:HALF, HALF:])
    right_ref[MODES:, :] = modes_of(blocks[HALF:, :HALF])
    left_ref[MODES:, :] = modes_of(blocks[HALF:, HALF:])


def updated(param, grad):
    rise = jnp.tanh(0.5 * param)
    return param - (step_rate / 4.0 / area) * (grad * (1.0 - rise * rise))


def columns_kernel(cols, own_left_ref, own_right_ref, left_ref, right_ref, even_ref, odd_ref):
    col = lax.axis_index("col")
    odd = lax.rem(lax.axis_index("row"), 2) == 1
    own = own_right_ref[...] + jnp.where(col < cols - 1, right_ref[...], 0.0)
    before = own_left_ref[...] + jnp.where(col > 0, left_ref[...], 0.0)
    below = jnp.concatenate([own[:MODES], before[:MODES]], 0)
    above = jnp.concatenate([own[MODES:], before[MODES:]], 0)
    by_parity(odd, even_ref, odd_ref, below, above)


def heal_kernel(
    rows, cols, first_ref, even_own_ref, odd_own_ref, even_ref, odd_ref, goal_ref, left_ref,
    right_ref, even_goal_ref, odd_goal_ref, resp_ref, swapped_ref, scaled_ref, cross_ref,
    weight_ref, edge_table_ref, table_ref, out_ref, field_ref,
):
    edge, t = Tables(edge_table_ref), Tables(table_ref)
    row, col = lax.axis_index("row"), lax.axis_index("col")
    odd = lax.rem(row, 2) == 1
    inner_row, inner_col = row < rows - 1, col < cols - 1
    lower, upper = below_above(odd, even_own_ref, odd_own_ref)
    below, above = below_above(odd, even_ref, odd_ref)
    lower = lower + jnp.where(inner_row, below, 0.0)
    upper = upper + jnp.where(row > 0, above, 0.0)
    own_goals = jnp.concatenate([left_ref[HALF:, :], goal_ref[...], right_ref[HALF:, :]], 1)
    goals_below, goals_above = below_above(odd, even_goal_ref, odd_goal_ref)
    goals_lower = jnp.concatenate([own_goals[HALF:].astype(F32), goals_below], 0)
    goals_upper = jnp.concatenate([goals_above, own_goals[:HALF].astype(F32)], 0)
    lower_right, lower_left, upper_right, upper_left = imaging_modes(
        [
            (lower[:MODES], goals_lower[:, TILE:], (inner_row, inner_col)),
            (lower[MODES:], goals_lower[:, :TILE], (inner_row, None)),
            (upper[:MODES], goals_upper[:, TILE:], (None, inner_col)),
            (upper[MODES:], goals_upper[:, :TILE], (None, None)),
        ],
        resp_ref, swapped_ref, scaled_ref, cross_ref, weight_ref, field_ref, t,
    )

    def kept(value, flag):
        return jnp.where(flag, value.astype(F32), 0.0).astype(BF16)

    left = jnp.concatenate(
        [kept(lower_left, col > 0), kept(upper_left, jnp.logical_and(row > 0, col > 0))], 0
    )
    right = jnp.concatenate([lower_right, kept(upper_right, row > 0)], 0)
    left = dot(left, t["inv_left"]).astype(BF16)
    right = dot(right, t["inv_right"]).astype(BF16)

    def quarter(modes):
        real = jnp.concatenate([left[modes, :HALF], right[modes, :HALF]], 1)
        imag = jnp.concatenate([left[modes, HALF:], right[modes, HALF:]], 1)
        return jnp.concatenate([real, imag], 0)

    q_inv = edge.right("own")
    below = dot(q_inv[:HALF], quarter(slice(0, MODES)))
    above = dot(q_inv[HALF:], quarter(slice(MODES, 2 * MODES)))
    out_ref[:HALF, :] = updated(first_ref[:HALF, :], above)
    out_ref[HALF:, :] = updated(first_ref[HALF:, :], below)


VMEM_SPEC = pl.BlockSpec(memory_space=VMEM)
SMEM_SPEC = pl.BlockSpec(memory_space=pltpu.SMEM)


def fields(windows):
    return [VMEM((windows * KERN, COARSE, 2 * COARSE), F32)]


def shape_of(rows, cols, dtype):
    return jax.ShapeDtypeStruct((rows, cols), dtype)


def per_device(rows, cols, mask_param, target, kernel_modes, kernel_weight):
    table, edge_table = jnp.asarray(MAIN_TABLE), jnp.asarray(EDGE_TABLE)

    def permuted(value, place):
        pairs = [
            (r * cols + c, place(r, c)[0] * cols + place(r, c)[1])
            for r in range(rows)
            for c in range(cols)
        ]
        return lax.ppermute(value, ("row", "col"), pairs)

    def move(value, down, right):
        return permuted(value, lambda r, c: ((r + down) % rows, (c + right) % cols))

    def swap(value, parity):
        def place(r, c):
            other = r + 1 if r % 2 == parity else r - 1
            return (other, c) if 0 <= other < rows else (r, c ^ 1)

        return permuted(value, place)

    def call(kernel, outs, other, limit, scratch, name, *args):
        return pl.pallas_call(
            kernel, out_shape=outs, in_specs=[other.get(i, VMEM_SPEC) for i in range(len(args))],
            out_specs=jax.tree.map(lambda _: VMEM_SPEC, outs), scratch_shapes=scratch,
            compiler_params=pltpu.CompilerParams(
                vmem_limit_bytes=limit
            ),
            name=name,
        )(*args)

    to_left, to_right, mask, goal = call(
        edges_kernel,
        (
            shape_of(HALF + TILE, HALF, BF16), shape_of(HALF + TILE, HALF, BF16),
            shape_of(TILE, TILE, F32), shape_of(TILE, TILE, BF16),
        ),
        {}, 4 << 20, (), "edges", mask_param, target,
    )
    edge_table = call(
        table_kernel, shape_of(*EDGE_TABLE.shape, BF16), {}, 4 << 20, (), "table",
        edge_table, to_right,
    )
    from_right = move(to_left, 0, -1)
    from_left = move(to_right, 0, 1)
    resp_shape = jax.ShapeDtypeStruct(kernel_modes.shape, F32)
    responses = call(
        responses_kernel, (resp_shape,) * 3 + (shape_of(KERN, COARSE, F32),), {1: SMEM_SPEC}, 4 << 20, (), "responses",
        kernel_modes, kernel_weight, to_right,
    )
    rim_shape, goal_shape = shape_of(MARGIN, 2 * MODES, BF16), shape_of(HALF, 2 * TILE, BF16)
    half_spec, even_rim, odd_rim, even_goal, odd_goal = call(
        lambda *refs: strip_kernel(cols, *refs),
        (shape_of(TILE, 2 * MODES, BF16), rim_shape, rim_shape, goal_shape, goal_shape),
        {}, 4 << 20, (), "strip", mask, goal, from_left, from_right, edge_table,
    )
    even_rim, odd_rim = swap(even_rim, 0), swap(odd_rim, 1)
    even_goal, odd_goal = swap(even_goal, 0), swap(odd_goal, 1)
    pair_shape = shape_of(2 * MODES, 2 * MODES, F32)
    first, to_left, to_right = call(
        lambda *refs: first_kernel(rows, *refs),
        (shape_of(TILE, TILE, F32), pair_shape, pair_shape), {}, 12 << 20, fields(1),
        "first", mask, half_spec, even_rim, odd_rim, goal, kernel_modes, *responses,
        edge_table, table,
    )
    even_own, odd_own = call(
        lambda *refs: columns_kernel(cols, *refs), (pair_shape, pair_shape), {}, 4 << 20, (),
        "columns", to_left, to_right, move(to_right, 0, 1), move(to_left, 0, -1),
    )
    return call(
        lambda *refs: heal_kernel(rows, cols, *refs), shape_of(TILE, TILE, F32),
        {}, 24 << 20, fields(4), "heal",
        first, even_own, odd_own, swap(even_own, 0), swap(odd_own, 1), goal, from_left,
        from_right, even_goal, odd_goal, kernel_modes, *responses, edge_table, table,
    )


def solution(mesh):
    rows, cols = mesh.shape["row"], mesh.shape["col"]
    tile = P(("grp", "row"), "col")
    return jax.shard_map(
        lambda *args: per_device(rows, cols, *args), mesh=mesh,
        in_specs=(tile, tile, P(), P()), out_specs=tile, check_vma=False,
    )
```

```python
import math

import jax
import jax.numpy as jnp
import numpy as np
from jax import lax
from jax.experimental import pallas as pl
from jax.experimental.pallas import tpu as pltpu
from jax.sharding import PartitionSpec as P


TILE = 256
MARGIN = 64
MODES = 64
KERN = 12
HALF = 128
WIN = 384
COARSE = 128
STEP = WIN // COARSE

threshold = 0.4
step_rate = 16.0
area = float(WIN * WIN)

VMEM = pltpu.VMEM
BF16 = jnp.bfloat16
F32 = jnp.float32


def tables():
    freq = np.arange(MODES) - MODES // 2
    angle = (2.0 * math.pi / WIN) * np.mod(freq[:, None] * np.arange(WIN)[None], WIN)
    cos, sin = np.cos(angle), np.sin(angle)
    stacked = np.concatenate([cos, sin], 0)
    forward = stacked.T
    core = slice(MARGIN, MARGIN + TILE)
    c_core, s_core = cos[:, core], sin[:, core]
    c_low, s_low = cos[:, ::STEP], sin[:, ::STEP]
    reach = HALF + MARGIN
    place_a = np.zeros((TILE, 2 * MODES))
    place_a[TILE - reach :] = forward[:reach]
    place_b = np.zeros((TILE, 2 * MODES))
    place_b[:reach] = forward[reach:]
    offset = np.arange(MARGIN, MARGIN + TILE)[:, None] - STEP * np.arange(COARSE)[None]
    orders = np.arange(1, 2 * MODES // 2)
    interp = 1.0 + 2.0 * np.cos((2.0 * math.pi / WIN) * orders[:, None, None] * offset[None]).sum(0)
    interp = (interp + np.cos((2.0 * math.pi / WIN) * MODES * offset)) / COARSE
    high = interp.astype(jnp.bfloat16).astype(np.float64)
    pad = np.zeros((COARSE, COARSE))
    table = dict(
        own=(forward[core], np.concatenate([c_core.T, -s_core.T], 1)),
        rim=(
            np.concatenate([forward[MARGIN + TILE :], forward[:MARGIN]], 0),
            np.concatenate([stacked[:, :MARGIN], stacked[:, MARGIN + TILE :]], 1),
        ),
        q_own=(stacked[:, core],),
        spread=(np.block([[c_low, s_low], [-s_low, c_low]]),),
        q_low=(np.concatenate([c_low.T, s_low.T], 1), pad),
        interp=(high, interp - high),
        interp_t=(np.concatenate([high.T, (interp - high).T], 0),),
        gather=(
            np.block(
                [[c_low.T, -s_low.T, -s_low.T, -c_low.T], [s_low.T, c_low.T, c_low.T, -s_low.T]]
            ),
        ),
        q_back=(c_low, s_low),
        inv_left=(np.block([[c_core[:, HALF:], s_core[:, HALF:]], [-s_core[:, HALF:], c_core[:, HALF:]]]),),
        inv_right=(np.block([[c_core[:, :HALF], s_core[:, :HALF]], [-s_core[:, :HALF], c_core[:, :HALF]]]),),
        place=(place_a, place_b),
        q_place=(np.concatenate([place_a.T, place_b.T], 0),),
    )
    table = {name: np.concatenate(value, 1) for name, value in table.items()}
    arrays, rows = [], {}
    for names in (("own", "rim"), tuple(name for name in table if name not in ("own", "rim"))):
        start = 0
        for name in names:
            rows[name] = slice(start, start + len(table[name]))
            start = rows[name].stop
        arrays.append(np.concatenate([table[name] for name in names], 0).astype(jnp.bfloat16))
    return arrays, rows


(EDGE_TABLE, MAIN_TABLE), TABLE_ROWS = tables()


class Tables:
    def __init__(self, ref):
        self.ref = ref

    def __getitem__(self, name):
        return self.ref[TABLE_ROWS[name], :]

    def left(self, name):
        return self.ref[TABLE_ROWS[name], :COARSE]

    def right(self, name):
        return self.ref[TABLE_ROWS[name], COARSE:]


def dot(left, right):
    return jnp.dot(left, right, preferred_element_type=F32)


def swap_halves(value):
    return pltpu.roll(value, MODES, axis=1)


def low_lanes(shape):
    return lax.broadcasted_iota(jnp.int32, shape, 1) < MODES


def modes_of(blocks):
    top, bottom = blocks[:MODES], swap_halves(blocks[MODES:])
    return jnp.where(low_lanes(top.shape), top - bottom, -(top + bottom)) / area


def imaging_modes(windows, resp_ref, swapped_ref, scaled_ref, cross_ref, weight_ref, field_ref, t):
    count = len(windows)
    low = low_lanes((MODES, 2 * MODES))
    cuts = 2 if count == 1 else 1
    groups = [range(i * KERN // cuts, (i + 1) * KERN // cuts) for i in range(cuts)]
    partials = []
    for spec, _, _ in windows:
        swapped = swap_halves(spec)
        spec_a = jnp.where(low, spec, swapped)
        spec_b = jnp.where(low, -swapped, spec)
        partial = []
        for group in groups:
            filtered = [(resp_ref[k] * spec_a + swapped_ref[k] * spec_b).astype(BF16) for k in group]
            spread = dot(jnp.concatenate(filtered, 0), t["spread"]).astype(BF16)
            partial += [spread[i * MODES : (i + 1) * MODES] for i in range(len(group))]
        partials.append(partial)
    levels = []
    for w, partial in enumerate(partials):
        level = jnp.zeros((COARSE, COARSE), F32)
        for k, part in enumerate(partial):
            real, imag = part[:, :COARSE], part[:, COARSE:]
            rotated = jnp.concatenate([part, jnp.concatenate([-imag, real], 1)], 0)
            field = dot(t.left("q_low"), rotated)
            field_ref[w * KERN + k] = field
            a_real, a_imag = field[:, :COARSE], field[:, COARSE:]
            level = level + weight_ref[k : k + 1, :] * (a_real * a_real + a_imag * a_imag)
        levels.append((2.0 * level - 2.0 * threshold).astype(BF16))
    halves = [dot(t["interp"], jnp.concatenate([level, level], 0)).astype(BF16) for level in levels]
    cores = [dot(jnp.concatenate([half, half], 1), t["interp_t"]) for half in halves]
    lows = []
    for core, (_, goal, inner) in zip(cores, windows):
        rise = jnp.tanh(core)
        core_grad = ((rise + (1.0 - 2.0 * goal.astype(F32))) * (1.0 - rise * rise)).astype(BF16)
        rows_low, cols_low = t["interp_t"][:COARSE], t.left("interp")
        inner_row, inner_col = inner
        if inner_row is not None:
            outer = jnp.where(inner_row, rows_low[:, HALF:].astype(F32), 0.0).astype(BF16)
            rows_low = jnp.concatenate([rows_low[:, :HALF], outer], 1)
        if inner_col is not None:
            outer = jnp.where(inner_col, cols_low[HALF:].astype(F32), 0.0).astype(BF16)
            cols_low = jnp.concatenate([cols_low[:HALF], outer], 0)
        lows.append((dot(rows_low, core_grad).astype(BF16), cols_low))
    lows = [dot(left, right) for left, right in lows]
    gathers = []
    for w, low_grad in enumerate(lows):
        both = jnp.concatenate([low_grad, low_grad], 1)
        gathered = []
        for group in groups:
            shaded = [(field_ref[w * KERN + k] * both).astype(BF16) for k in group]
            rows = dot(jnp.concatenate(shaded, 0), t["gather"]).astype(BF16)
            gathered += [rows[i * COARSE : (i + 1) * COARSE] for i in range(len(group))]
        gathers.append(gathered)
    results = []
    for gathered in gathers:
        direct = jnp.zeros((MODES, 2 * MODES), F32)
        crossed = jnp.zeros((MODES, 2 * MODES), F32)
        for k in range(0, KERN, 2):
            one, two = gathered[k], gathered[k + 1]
            upper = jnp.concatenate([one[:, :COARSE], two[:, :COARSE]], 1)
            lower = jnp.concatenate([one[:, COARSE:], two[:, COARSE:]], 1)
            back = dot(t["q_back"], jnp.concatenate([upper, lower], 0))
            for i, part in enumerate((back[:, : 2 * MODES], back[:, 2 * MODES :])):
                direct = direct + scaled_ref[k + i] * part
                crossed = crossed + cross_ref[k + i] * part
        results.append(
            jnp.where(low, direct + swap_halves(direct), crossed - swap_halves(crossed)).astype(BF16)
        )
    return results


def edges_kernel(mask_ref, left_ref, right_ref, mask_out_ref):
    low = low_lanes((TILE, 2 * MARGIN))
    edge = jax.nn.sigmoid(jnp.where(low, mask_ref[:, : 2 * MARGIN], mask_ref[:, HALF:]))
    top, bottom = edge[:HALF], edge[HALF:]
    low = low[:HALF]
    left_ref[...] = jnp.where(low, top, swap_halves(bottom)).astype(BF16)
    right_ref[...] = jnp.where(low, swap_halves(top), bottom).astype(BF16)
    mask_out_ref[...] = mask_ref[...]


def goals_kernel(target_ref, after_ref, left_ref, right_ref, target_out_ref):
    left_ref[...] = target_ref[:, :HALF]
    right_ref[...] = target_ref[:, HALF:]
    target_out_ref[...] = target_ref[...]


def table_kernel(table_ref, kernel_weight_ref, after_ref, out_ref, weight_ref):
    out_ref[...] = table_ref[...]
    weights = kernel_weight_ref[...]
    for k in range(KERN):
        weight_ref[k : k + 1, :] = jnp.broadcast_to(weights[:, k : k + 1], (1, COARSE))


def by_parity(odd, even_ref, odd_ref, below, above):
    @pl.when(odd)
    def _():
        even_ref[...] = above
        odd_ref[...] = below

    @pl.when(jnp.logical_not(odd))
    def _():
        even_ref[...] = below
        odd_ref[...] = above


def below_above(odd, even_ref, odd_ref):
    even, odd_value = even_ref[...].astype(F32), odd_ref[...].astype(F32)
    return jnp.where(odd, odd_value, even), jnp.where(odd, even, odd_value)


def strip_kernel(cols, mask_ref, left_ref, right_ref, table_ref, u_ref, even_ref, odd_ref):
    t = Tables(table_ref)
    col = lax.axis_index("col")
    odd = lax.rem(lax.axis_index("row"), 2) == 1
    wire = jax.nn.sigmoid(mask_ref[...]).astype(BF16)
    low = low_lanes((HALF, 2 * MARGIN))
    right = jnp.where(col < cols - 1, right_ref[...].astype(F32), 0.0)
    left = jnp.where(col > 0, left_ref[...].astype(F32), 0.0)
    rim = jnp.concatenate(
        [jnp.where(low, right, swap_halves(left)), jnp.where(low, swap_halves(right), left)], 0
    ).astype(BF16)
    half_spec = (dot(wire, t.left("own")) + dot(rim, t.left("rim"))).astype(BF16)
    u_ref[...] = half_spec
    by_parity(odd, even_ref, odd_ref, half_spec[TILE - MARGIN :], half_spec[:MARGIN])


def goal_rows_kernel(target_ref, left_ref, right_ref, after_ref, even_ref, odd_ref):
    odd = lax.rem(lax.axis_index("row"), 2) == 1
    goals = jnp.concatenate([left_ref[...], target_ref[...], right_ref[...]], 1)
    by_parity(odd, even_ref, odd_ref, goals[HALF:], goals[:HALF])


def first_kernel(
    rows, mask_ref, u_ref, even_ref, odd_ref, goal_ref, resp_ref, weight_ref,
    edge_table_ref, table_ref, first_ref, left_ref, right_ref, swapped_ref, scaled_ref, cross_ref,
    field_ref,
):
    for k in range(KERN):
        weight = weight_ref[k : k + 1, :]
        swapped = swap_halves(resp_ref[k])
        swapped_ref[k] = swapped
        scaled_ref[k] = (2.0 * weight) * resp_ref[k]
        cross_ref[k] = (2.0 * weight) * swapped
    edge, t = Tables(edge_table_ref), Tables(table_ref)
    row = lax.axis_index("row")
    below, above = below_above(lax.rem(row, 2) == 1, even_ref, odd_ref)
    above = jnp.where(row > 0, above, 0.0)
    below = jnp.where(row < rows - 1, below, 0.0)
    rim = jnp.concatenate([above, below], 0).astype(BF16)
    spec = modes_of(dot(t["q_own"], u_ref[...]) + dot(edge.right("rim"), rim))
    (combined,) = imaging_modes(
        [(spec, goal_ref[...], (None, None))], resp_ref, swapped_ref, scaled_ref, cross_ref,
        weight_ref, field_ref, t,
    )
    left = dot(combined, t["inv_right"]).astype(BF16)
    right = dot(combined, t["inv_left"]).astype(BF16)
    real = jnp.concatenate([left[:, :HALF], right[:, :HALF]], 1)
    imag = jnp.concatenate([left[:, HALF:], right[:, HALF:]], 1)
    mask_grad = dot(edge.right("own"), jnp.concatenate([real, imag], 0))
    mask = mask_ref[...]
    first = updated(mask, mask_grad)
    first_ref[...] = first
    half = dot(jax.nn.sigmoid(first).astype(BF16), t["place"])
    half_hi = half.astype(BF16)
    half_lo = (half - half_hi.astype(F32)).astype(BF16)
    blocks = dot(t["q_place"], half_hi) + dot(t["q_place"], half_lo)
    right_ref[:MODES, :] = modes_of(blocks[:HALF, :HALF])
    left_ref[:MODES, :] = modes_of(blocks[:HALF, HALF:])
    right_ref[MODES:, :] = modes_of(blocks[HALF:, :HALF])
    left_ref[MODES:, :] = modes_of(blocks[HALF:, HALF:])


def updated(param, grad):
    rise = jnp.tanh(0.5 * param)
    return param - (step_rate / 4.0 / area) * (grad * (1.0 - rise * rise))


def columns_kernel(cols, own_left_ref, own_right_ref, left_ref, right_ref, even_ref, odd_ref):
    col = lax.axis_index("col")
    odd = lax.rem(lax.axis_index("row"), 2) == 1
    own = own_right_ref[...] + jnp.where(col < cols - 1, right_ref[...], 0.0)
    before = own_left_ref[...] + jnp.where(col > 0, left_ref[...], 0.0)
    below = jnp.concatenate([own[:MODES], before[:MODES]], 0)
    above = jnp.concatenate([own[MODES:], before[MODES:]], 0)
    by_parity(odd, even_ref, odd_ref, below, above)


def heal_kernel(
    rows, cols, first_ref, even_own_ref, odd_own_ref, even_ref, odd_ref, goal_ref, left_ref,
    right_ref, even_goal_ref, odd_goal_ref, resp_ref, swapped_ref, scaled_ref, cross_ref,
    weight_ref, edge_table_ref, table_ref, out_ref, field_ref,
):
    edge, t = Tables(edge_table_ref), Tables(table_ref)
    row, col = lax.axis_index("row"), lax.axis_index("col")
    odd = lax.rem(row, 2) == 1
    inner_row, inner_col = row < rows - 1, col < cols - 1
    lower, upper = below_above(odd, even_own_ref, odd_own_ref)
    below, above = below_above(odd, even_ref, odd_ref)
    lower = lower + jnp.where(inner_row, below, 0.0)
    upper = upper + jnp.where(row > 0, above, 0.0)
    own_goals = jnp.concatenate([left_ref[...], goal_ref[...], right_ref[...]], 1)
    goals_below, goals_above = below_above(odd, even_goal_ref, odd_goal_ref)
    goals_lower = jnp.concatenate([own_goals[HALF:].astype(F32), goals_below], 0)
    goals_upper = jnp.concatenate([goals_above, own_goals[:HALF].astype(F32)], 0)
    lower_right, lower_left, upper_right, upper_left = imaging_modes(
        [
            (lower[:MODES], goals_lower[:, TILE:], (inner_row, inner_col)),
            (lower[MODES:], goals_lower[:, :TILE], (inner_row, None)),
            (upper[:MODES], goals_upper[:, TILE:], (None, inner_col)),
            (upper[MODES:], goals_upper[:, :TILE], (None, None)),
        ],
        resp_ref, swapped_ref, scaled_ref, cross_ref, weight_ref, field_ref, t,
    )

    def kept(value, flag):
        return jnp.where(flag, value.astype(F32), 0.0).astype(BF16)

    left = jnp.concatenate(
        [kept(lower_left, col > 0), kept(upper_left, jnp.logical_and(row > 0, col > 0))], 0
    )
    right = jnp.concatenate([lower_right, kept(upper_right, row > 0)], 0)
    left = dot(left, t["inv_left"]).astype(BF16)
    right = dot(right, t["inv_right"]).astype(BF16)

    def quarter(modes):
        real = jnp.concatenate([left[modes, :HALF], right[modes, :HALF]], 1)
        imag = jnp.concatenate([left[modes, HALF:], right[modes, HALF:]], 1)
        return jnp.concatenate([real, imag], 0)

    q_inv = edge.right("own")
    below = dot(q_inv[:HALF], quarter(slice(0, MODES)))
    above = dot(q_inv[HALF:], quarter(slice(MODES, 2 * MODES)))
    out_ref[:HALF, :] = updated(first_ref[:HALF, :], above)
    out_ref[HALF:, :] = updated(first_ref[HALF:, :], below)


COST = {
    name: pl.CostEstimate(flops=int(micros * 1.1e9), bytes_accessed=1 << 16, transcendentals=0)
    for name, micros in (
        ("edges", 1.0), ("goals", 1.0), ("table", 1.0), ("strip", 1.0), ("goal_rows", 1.0),
        ("first", 3.0), ("columns", 1.0), ("heal", 5.0),
    )
}
VMEM_SPEC = pl.BlockSpec(memory_space=VMEM)
SMEM_SPEC = pl.BlockSpec(memory_space=pltpu.SMEM)


def fields(windows):
    return [VMEM((windows * KERN, COARSE, 2 * COARSE), F32)]


def shape_of(rows, cols, dtype):
    return jax.ShapeDtypeStruct((rows, cols), dtype)


def per_device(rows, cols, mask_param, target, kernel_modes, kernel_weight):
    table, edge_table = jnp.asarray(MAIN_TABLE), jnp.asarray(EDGE_TABLE)

    def permuted(value, place):
        pairs = [
            (r * cols + c, place(r, c)[0] * cols + place(r, c)[1])
            for r in range(rows)
            for c in range(cols)
        ]
        return lax.ppermute(value, ("row", "col"), pairs)

    def move(value, down, right):
        return permuted(value, lambda r, c: ((r + down) % rows, (c + right) % cols))

    def swap(value, parity):
        def place(r, c):
            other = r + 1 if r % 2 == parity else r - 1
            return (other, c) if 0 <= other < rows else (r, c ^ 1)

        return permuted(value, place)

    def call(kernel, outs, other, limit, scratch, name, *args):
        return pl.pallas_call(
            kernel, out_shape=outs, in_specs=[other.get(i, VMEM_SPEC) for i in range(len(args))],
            out_specs=jax.tree.map(lambda _: VMEM_SPEC, outs), scratch_shapes=scratch,
            compiler_params=pltpu.CompilerParams(vmem_limit_bytes=limit),
            cost_estimate=COST[name],
        )(*args)

    edge_shape = shape_of(HALF, 2 * MARGIN, BF16)
    to_left, to_right, mask = call(
        edges_kernel, (edge_shape, edge_shape, shape_of(TILE, TILE, F32)), {}, 4 << 20, (),
        "edges", mask_param,
    )
    from_right = move(to_left, 0, -1)
    from_left = move(to_right, 0, 1)
    goal_shape = shape_of(TILE, HALF, BF16)
    goal_left, goal_right, goal = call(
        goals_kernel, (goal_shape, goal_shape, shape_of(TILE, TILE, BF16)), {}, 4 << 20, (),
        "goals", target, to_right,
    )
    goal_right, goal_left = move(goal_left, 0, -1), move(goal_right, 0, 1)
    edge_table, weights = call(
        table_kernel, (shape_of(*EDGE_TABLE.shape, BF16), shape_of(KERN, COARSE, F32)), {},
        4 << 20, (), "table", edge_table, kernel_weight.reshape(1, KERN), to_right,
    )
    rim_shape = shape_of(MARGIN, 2 * MODES, BF16)
    half_spec, even_rim, odd_rim = call(
        lambda *refs: strip_kernel(cols, *refs),
        (shape_of(TILE, 2 * MODES, BF16), rim_shape, rim_shape), {}, 4 << 20, (), "strip",
        mask, from_left, from_right, edge_table,
    )
    goal_shape = shape_of(HALF, 2 * TILE, BF16)
    even_goal, odd_goal = call(
        goal_rows_kernel, (goal_shape, goal_shape), {}, 4 << 20, (), "goal_rows",
        goal, goal_left, goal_right, even_rim,
    )
    even_rim, odd_rim = swap(even_rim, 0), swap(odd_rim, 1)
    even_goal, odd_goal = swap(even_goal, 0), swap(odd_goal, 1)
    pair_shape = shape_of(2 * MODES, 2 * MODES, F32)
    resp_shape = jax.ShapeDtypeStruct(kernel_modes.shape, F32)
    first, to_left, to_right, *responses = call(
        lambda *refs: first_kernel(rows, *refs),
        (shape_of(TILE, TILE, F32), pair_shape, pair_shape)
        + (resp_shape,) * 3,
        {}, 16 << 20, fields(1), "first", mask, half_spec, even_rim, odd_rim, goal, kernel_modes,
        weights, edge_table, table,
    )
    even_own, odd_own = call(
        lambda *refs: columns_kernel(cols, *refs), (pair_shape, pair_shape), {}, 4 << 20, (),
        "columns", to_left, to_right, move(to_right, 0, 1), move(to_left, 0, -1),
    )
    return call(
        lambda *refs: heal_kernel(rows, cols, *refs), shape_of(TILE, TILE, F32),
        {}, 24 << 20, fields(4), "heal",
        first, even_own, odd_own, swap(even_own, 0), swap(odd_own, 1), goal, goal_left,
        goal_right, even_goal, odd_goal, kernel_modes, *responses, weights, edge_table,
        table,
    )


def solution(mesh):
    rows, cols = mesh.shape["row"], mesh.shape["col"]
    tile = P(("grp", "row"), "col")

    def body(*args):
        return per_device(rows, cols, *args)

    return jax.shard_map(
        body, mesh=mesh, in_specs=(tile, tile, P(), P()), out_specs=tile, check_vma=False
    )
```

```python
import math

import jax
import jax.numpy as jnp
import numpy as np
from jax import lax
from jax.experimental import pallas as pl
from jax.experimental.pallas import tpu as pltpu
from jax.sharding import PartitionSpec as P


TILE = 256
MARGIN = 64
MODES = 64
KERN = 12
HALF = 128
WIN = 384
COARSE = 128
STEP = WIN // COARSE

threshold = 0.4
step_rate = 16.0
area = float(WIN * WIN)

VMEM = pltpu.VMEM
BF16 = jnp.bfloat16
F32 = jnp.float32


def tables():
    freq = np.arange(MODES) - MODES // 2
    angle = (2.0 * math.pi / WIN) * np.mod(freq[:, None] * np.arange(WIN)[None], WIN)
    cos, sin = np.cos(angle), np.sin(angle)
    stacked = np.concatenate([cos, sin], 0)
    forward = stacked.T
    core = slice(MARGIN, MARGIN + TILE)
    c_core, s_core = cos[:, core], sin[:, core]
    c_low, s_low = cos[:, ::STEP], sin[:, ::STEP]
    reach = HALF + MARGIN
    place_a = np.zeros((TILE, 2 * MODES))
    place_a[TILE - reach :] = forward[:reach]
    place_b = np.zeros((TILE, 2 * MODES))
    place_b[:reach] = forward[reach:]
    offset = np.arange(MARGIN, MARGIN + TILE)[:, None] - STEP * np.arange(COARSE)[None]
    orders = np.arange(1, 2 * MODES // 2)
    interp = 1.0 + 2.0 * np.cos((2.0 * math.pi / WIN) * orders[:, None, None] * offset[None]).sum(0)
    interp = (interp + np.cos((2.0 * math.pi / WIN) * MODES * offset)) / COARSE
    high = interp.astype(jnp.bfloat16).astype(np.float64)
    pad = np.zeros((COARSE, COARSE))
    table = dict(
        own=(forward[core], np.concatenate([c_core.T, -s_core.T], 1)),
        rim=(
            np.concatenate([forward[MARGIN + TILE :], forward[:MARGIN]], 0),
            np.concatenate([stacked[:, :MARGIN], stacked[:, MARGIN + TILE :]], 1),
        ),
        q_own=(stacked[:, core],),
        spread=(np.block([[c_low, s_low], [-s_low, c_low]]),),
        q_low=(np.concatenate([c_low.T, s_low.T], 1), pad),
        interp=(high, interp - high),
        interp_t=(np.concatenate([high.T, (interp - high).T], 0),),
        gather=(
            np.block(
                [[c_low.T, -s_low.T, -s_low.T, -c_low.T], [s_low.T, c_low.T, c_low.T, -s_low.T]]
            ),
        ),
        q_back=(c_low, s_low),
        inv_left=(np.block([[c_core[:, HALF:], s_core[:, HALF:]], [-s_core[:, HALF:], c_core[:, HALF:]]]),),
        inv_right=(np.block([[c_core[:, :HALF], s_core[:, :HALF]], [-s_core[:, :HALF], c_core[:, :HALF]]]),),
        place=(place_a, place_b),
        q_place=(np.concatenate([place_a.T, place_b.T], 0),),
    )
    table = {name: np.concatenate(value, 1) for name, value in table.items()}
    arrays, rows = [], {}
    for names in (("own", "rim"), tuple(name for name in table if name not in ("own", "rim"))):
        start = 0
        for name in names:
            rows[name] = slice(start, start + len(table[name]))
            start = rows[name].stop
        arrays.append(np.concatenate([table[name] for name in names], 0).astype(jnp.bfloat16))
    place = table["place"].astype(jnp.bfloat16).astype(np.float64)
    sums = 0.5 * place.sum(0)
    level = []
    for q in (place[:, : 2 * MODES].sum(0), place[:, 2 * MODES :].sum(0)):
        for t in (sums[: 2 * MODES], sums[2 * MODES :]):
            c, s = slice(0, MODES), slice(MODES, 2 * MODES)
            real = np.outer(q[c], t[c]) - np.outer(q[s], t[s])
            imag = -np.outer(q[c], t[s]) - np.outer(q[s], t[c])
            level.append(np.concatenate([real, imag], 1) / area)
    level.append(np.concatenate([sums.reshape(2, 2 * MODES), np.zeros((6, 2 * MODES))], 0))
    return arrays + [np.concatenate(level, 0).astype(np.float32)], rows


(EDGE_TABLE, MAIN_TABLE, LEVEL_TABLE), TABLE_ROWS = tables()


class Tables:
    def __init__(self, ref):
        self.ref = ref

    def __getitem__(self, name):
        return self.ref[TABLE_ROWS[name], :]

    def left(self, name):
        return self.ref[TABLE_ROWS[name], :COARSE]

    def right(self, name):
        return self.ref[TABLE_ROWS[name], COARSE:]


def dot(left, right):
    return jnp.dot(left, right, preferred_element_type=F32)


def swap_halves(value):
    return pltpu.roll(value, MODES, axis=1)


def low_lanes(shape):
    return lax.broadcasted_iota(jnp.int32, shape, 1) < MODES


def modes_of(blocks):
    top, bottom = blocks[:MODES], swap_halves(blocks[MODES:])
    return jnp.where(low_lanes(top.shape), top - bottom, -(top + bottom)) / area


def imaging_modes(windows, resp_ref, swapped_ref, scaled_ref, cross_ref, weight_ref, field_ref, t):
    count = len(windows)
    low = low_lanes((MODES, 2 * MODES))
    cuts = 2 if count == 1 else 1
    groups = [range(i * KERN // cuts, (i + 1) * KERN // cuts) for i in range(cuts)]
    partials = []
    for spec, _, _ in windows:
        swapped = swap_halves(spec)
        spec_a = jnp.where(low, spec, swapped)
        spec_b = jnp.where(low, -swapped, spec)
        partial = []
        for group in groups:
            filtered = [(resp_ref[k] * spec_a + swapped_ref[k] * spec_b).astype(BF16) for k in group]
            spread = dot(jnp.concatenate(filtered, 0), t["spread"]).astype(BF16)
            partial += [spread[i * MODES : (i + 1) * MODES] for i in range(len(group))]
        partials.append(partial)
    levels = []
    for w, partial in enumerate(partials):
        chains = [jnp.zeros((COARSE, COARSE), F32)] * 2
        for k, part in enumerate(partial):
            real, imag = part[:, :COARSE], part[:, COARSE:]
            rotated = jnp.concatenate([part, jnp.concatenate([-imag, real], 1)], 0)
            field = dot(t.left("q_low"), rotated)
            field_ref[w * KERN + k] = field
            a_real, a_imag = field[:, :COARSE], field[:, COARSE:]
            chains[k % 2] = chains[k % 2] + weight_ref[k : k + 1, :] * (
                a_real * a_real + a_imag * a_imag
            )
        level = chains[0] + chains[1]
        levels.append((2.0 * level - 2.0 * threshold).astype(BF16))
    halves = [dot(t["interp"], jnp.concatenate([level, level], 0)).astype(BF16) for level in levels]
    cores = [dot(jnp.concatenate([half, half], 1), t["interp_t"]) for half in halves]
    lows = []
    for core, (_, goal, inner) in zip(cores, windows):
        rise = jnp.tanh(core)
        core_grad = ((rise + (1.0 - 2.0 * goal.astype(F32))) * (1.0 - rise * rise)).astype(BF16)
        rows_low, cols_low = t["interp_t"][:COARSE], t.left("interp")
        inner_row, inner_col = inner
        if inner_row is not None:
            outer = jnp.where(inner_row, rows_low[:, HALF:].astype(F32), 0.0).astype(BF16)
            rows_low = jnp.concatenate([rows_low[:, :HALF], outer], 1)
        if inner_col is not None:
            outer = jnp.where(inner_col, cols_low[HALF:].astype(F32), 0.0).astype(BF16)
            cols_low = jnp.concatenate([cols_low[:HALF], outer], 0)
        lows.append((dot(rows_low, core_grad).astype(BF16), cols_low))
    lows = [dot(left, right) for left, right in lows]
    gathers = []
    for w, low_grad in enumerate(lows):
        both = jnp.concatenate([low_grad, low_grad], 1)
        gathered = []
        for group in groups:
            shaded = [(field_ref[w * KERN + k] * both).astype(BF16) for k in group]
            rows = dot(jnp.concatenate(shaded, 0), t["gather"]).astype(BF16)
            gathered += [rows[i * COARSE : (i + 1) * COARSE] for i in range(len(group))]
        gathers.append(gathered)
    results = []
    for gathered in gathers:
        direct = jnp.zeros((MODES, 2 * MODES), F32)
        crossed = jnp.zeros((MODES, 2 * MODES), F32)
        for k in range(0, KERN, 2):
            one, two = gathered[k], gathered[k + 1]
            upper = jnp.concatenate([one[:, :COARSE], two[:, :COARSE]], 1)
            lower = jnp.concatenate([one[:, COARSE:], two[:, COARSE:]], 1)
            back = dot(t["q_back"], jnp.concatenate([upper, lower], 0))
            for i, part in enumerate((back[:, : 2 * MODES], back[:, 2 * MODES :])):
                direct = direct + scaled_ref[k + i] * part
                crossed = crossed + cross_ref[k + i] * part
        results.append(
            jnp.where(low, direct + swap_halves(direct), crossed - swap_halves(crossed)).astype(BF16)
        )
    return results


def edges_kernel(mask_ref, left_ref, right_ref, mask_out_ref):
    low = low_lanes((TILE, 2 * MARGIN))
    edge = jax.nn.sigmoid(jnp.where(low, mask_ref[:, : 2 * MARGIN], mask_ref[:, HALF:]))
    top, bottom = edge[:HALF], edge[HALF:]
    low = low[:HALF]
    left_ref[...] = jnp.where(low, top, swap_halves(bottom)).astype(BF16)
    right_ref[...] = jnp.where(low, swap_halves(top), bottom).astype(BF16)
    mask_out_ref[...] = mask_ref[...]


def goals_kernel(target_ref, after_ref, left_ref, right_ref, target_out_ref):
    left_ref[...] = target_ref[:, :HALF]
    right_ref[...] = target_ref[:, HALF:]
    target_out_ref[...] = target_ref[...]


def table_kernel(table_ref, kernel_weight_ref, after_ref, out_ref, weight_ref):
    out_ref[...] = table_ref[...]
    weights = kernel_weight_ref[...]
    for k in range(KERN):
        weight_ref[k : k + 1, :] = jnp.broadcast_to(weights[:, k : k + 1], (1, COARSE))


def by_parity(odd, even_ref, odd_ref, below, above):
    @pl.when(odd)
    def _():
        even_ref[...] = above
        odd_ref[...] = below

    @pl.when(jnp.logical_not(odd))
    def _():
        even_ref[...] = below
        odd_ref[...] = above


def below_above(odd, even_ref, odd_ref):
    even, odd_value = even_ref[...].astype(F32), odd_ref[...].astype(F32)
    return jnp.where(odd, odd_value, even), jnp.where(odd, even, odd_value)


def strip_kernel(cols, mask_ref, left_ref, right_ref, table_ref, u_ref, even_ref, odd_ref):
    t = Tables(table_ref)
    col = lax.axis_index("col")
    odd = lax.rem(lax.axis_index("row"), 2) == 1
    wire = jax.nn.sigmoid(mask_ref[...]).astype(BF16)
    low = low_lanes((HALF, 2 * MARGIN))
    right = jnp.where(col < cols - 1, right_ref[...].astype(F32), 0.0)
    left = jnp.where(col > 0, left_ref[...].astype(F32), 0.0)
    rim = jnp.concatenate(
        [jnp.where(low, right, swap_halves(left)), jnp.where(low, swap_halves(right), left)], 0
    ).astype(BF16)
    half_spec = (dot(wire, t.left("own")) + dot(rim, t.left("rim"))).astype(BF16)
    u_ref[...] = half_spec
    by_parity(odd, even_ref, odd_ref, half_spec[TILE - MARGIN :], half_spec[:MARGIN])


def goal_rows_kernel(target_ref, left_ref, right_ref, after_ref, even_ref, odd_ref):
    odd = lax.rem(lax.axis_index("row"), 2) == 1
    goals = jnp.concatenate([left_ref[...], target_ref[...], right_ref[...]], 1)
    by_parity(odd, even_ref, odd_ref, goals[HALF:], goals[:HALF])


def first_kernel(
    rows, mask_ref, u_ref, even_ref, odd_ref, goal_ref, resp_ref, weight_ref,
    edge_table_ref, table_ref, level_ref, first_ref, left_ref, right_ref, swapped_ref, scaled_ref, cross_ref,
    field_ref,
):
    for k in range(KERN):
        weight = weight_ref[k : k + 1, :]
        swapped = swap_halves(resp_ref[k])
        swapped_ref[k] = swapped
        scaled_ref[k] = (2.0 * weight) * resp_ref[k]
        cross_ref[k] = (2.0 * weight) * swapped
    edge, t = Tables(edge_table_ref), Tables(table_ref)
    row = lax.axis_index("row")
    below, above = below_above(lax.rem(row, 2) == 1, even_ref, odd_ref)
    above = jnp.where(row > 0, above, 0.0)
    below = jnp.where(row < rows - 1, below, 0.0)
    rim = jnp.concatenate([above, below], 0).astype(BF16)
    spec = modes_of(dot(t["q_own"], u_ref[...]) + dot(edge.right("rim"), rim))
    (combined,) = imaging_modes(
        [(spec, goal_ref[...], (None, None))], resp_ref, swapped_ref, scaled_ref, cross_ref,
        weight_ref, field_ref, t,
    )
    left = dot(combined, t["inv_right"]).astype(BF16)
    right = dot(combined, t["inv_left"]).astype(BF16)
    real = jnp.concatenate([left[:, :HALF], right[:, :HALF]], 1)
    imag = jnp.concatenate([left[:, HALF:], right[:, HALF:]], 1)
    mask_grad = dot(edge.right("own"), jnp.concatenate([real, imag], 0))
    mask = mask_ref[...]
    first = updated(mask, mask_grad)
    first_ref[...] = first
    sums = jnp.concatenate([level_ref[4 * MODES : 4 * MODES + 1, :], level_ref[4 * MODES + 1 : 4 * MODES + 2, :]], 1)
    half = dot(jax.nn.sigmoid(first).astype(BF16), t["place"]) - sums
    blocks = dot(t["q_place"], half.astype(BF16))
    right_ref[:MODES, :] = modes_of(blocks[:HALF, :HALF]).astype(BF16)
    left_ref[:MODES, :] = modes_of(blocks[:HALF, HALF:]).astype(BF16)
    right_ref[MODES:, :] = modes_of(blocks[HALF:, :HALF]).astype(BF16)
    left_ref[MODES:, :] = modes_of(blocks[HALF:, HALF:]).astype(BF16)


def updated(param, grad):
    rise = jnp.tanh(0.5 * param)
    return param - (step_rate / 4.0 / area) * (grad * (1.0 - rise * rise))


def columns_kernel(cols, own_left_ref, own_right_ref, left_ref, right_ref, even_ref, odd_ref):
    col = lax.axis_index("col")
    odd = lax.rem(lax.axis_index("row"), 2) == 1
    own = own_right_ref[...].astype(F32) + jnp.where(col < cols - 1, right_ref[...].astype(F32), 0.0)
    before = own_left_ref[...].astype(F32) + jnp.where(col > 0, left_ref[...].astype(F32), 0.0)
    below = jnp.concatenate([own[:MODES], before[:MODES]], 0).astype(BF16)
    above = jnp.concatenate([own[MODES:], before[MODES:]], 0).astype(BF16)
    by_parity(odd, even_ref, odd_ref, below, above)


def heal_kernel(
    rows, cols, first_ref, even_own_ref, odd_own_ref, even_ref, odd_ref, goal_ref, left_ref,
    right_ref, even_goal_ref, odd_goal_ref, resp_ref, swapped_ref, scaled_ref, cross_ref,
    weight_ref, edge_table_ref, table_ref, level_ref, out_ref, field_ref,
):
    edge, t = Tables(edge_table_ref), Tables(table_ref)
    row, col = lax.axis_index("row"), lax.axis_index("col")
    odd = lax.rem(row, 2) == 1
    inner_row, inner_col = row < rows - 1, col < cols - 1
    lower, upper = below_above(odd, even_own_ref, odd_own_ref)
    below, above = below_above(odd, even_ref, odd_ref)
    lower = lower + jnp.where(inner_row, below, 0.0)
    upper = upper + jnp.where(row > 0, above, 0.0)
    aa, ab, ba, bb = (level_ref[i * MODES : (i + 1) * MODES, :] for i in range(4))
    own_columns = aa + jnp.where(inner_col, ab, 0.0), ba + jnp.where(inner_col, bb, 0.0)
    both_columns = aa + ab, ba + bb
    lower = lower + jnp.concatenate(
        [a + jnp.where(inner_row, b, 0.0) for a, b in (own_columns, both_columns)], 0
    )
    upper = upper + jnp.concatenate([a + b for a, b in (own_columns, both_columns)], 0)
    own_goals = jnp.concatenate([left_ref[...], goal_ref[...], right_ref[...]], 1)
    goals_below, goals_above = below_above(odd, even_goal_ref, odd_goal_ref)
    goals_lower = jnp.concatenate([own_goals[HALF:].astype(F32), goals_below], 0)
    goals_upper = jnp.concatenate([goals_above, own_goals[:HALF].astype(F32)], 0)
    lower_right, lower_left, upper_right, upper_left = imaging_modes(
        [
            (lower[:MODES], goals_lower[:, TILE:], (inner_row, inner_col)),
            (lower[MODES:], goals_lower[:, :TILE], (inner_row, None)),
            (upper[:MODES], goals_upper[:, TILE:], (None, inner_col)),
            (upper[MODES:], goals_upper[:, :TILE], (None, None)),
        ],
        resp_ref, swapped_ref, scaled_ref, cross_ref, weight_ref, field_ref, t,
    )

    def kept(value, flag):
        return jnp.where(flag, value.astype(F32), 0.0).astype(BF16)

    left = jnp.concatenate(
        [kept(lower_left, col > 0), kept(upper_left, jnp.logical_and(row > 0, col > 0))], 0
    )
    right = jnp.concatenate([lower_right, kept(upper_right, row > 0)], 0)
    left = dot(left, t["inv_left"]).astype(BF16)
    right = dot(right, t["inv_right"]).astype(BF16)

    def quarter(modes):
        real = jnp.concatenate([left[modes, :HALF], right[modes, :HALF]], 1)
        imag = jnp.concatenate([left[modes, HALF:], right[modes, HALF:]], 1)
        return jnp.concatenate([real, imag], 0)

    q_inv = edge.right("own")
    below = dot(q_inv[:HALF], quarter(slice(0, MODES)))
    above = dot(q_inv[HALF:], quarter(slice(MODES, 2 * MODES)))
    out_ref[:HALF, :] = updated(first_ref[:HALF, :], above)
    out_ref[HALF:, :] = updated(first_ref[HALF:, :], below)


COST = {
    name: pl.CostEstimate(flops=int(micros * 1.1e9), bytes_accessed=1 << 16, transcendentals=0)
    for name, micros in (
        ("edges", 1.0), ("goals", 1.0), ("table", 1.0), ("strip", 1.0), ("goal_rows", 1.0),
        ("first", 3.0), ("columns", 1.0), ("heal", 5.0),
    )
}
VMEM_SPEC = pl.BlockSpec(memory_space=VMEM)
SMEM_SPEC = pl.BlockSpec(memory_space=pltpu.SMEM)


def fields(windows):
    return [VMEM((windows * KERN, COARSE, 2 * COARSE), F32)]


def shape_of(rows, cols, dtype):
    return jax.ShapeDtypeStruct((rows, cols), dtype)


def per_device(rows, cols, mask_param, target, kernel_modes, kernel_weight):
    table, edge_table = jnp.asarray(MAIN_TABLE), jnp.asarray(EDGE_TABLE)
    level = jnp.asarray(LEVEL_TABLE)

    def permuted(value, place):
        pairs = [
            (r * cols + c, place(r, c)[0] * cols + place(r, c)[1])
            for r in range(rows)
            for c in range(cols)
        ]
        return lax.ppermute(value, ("row", "col"), pairs)

    def move(value, down, right):
        return permuted(value, lambda r, c: ((r + down) % rows, (c + right) % cols))

    def swap(value, parity):
        def place(r, c):
            other = r + 1 if r % 2 == parity else r - 1
            return (other, c) if 0 <= other < rows else (r, c ^ 1)

        return permuted(value, place)

    def call(kernel, outs, other, limit, scratch, name, *args):
        return pl.pallas_call(
            kernel, out_shape=outs, in_specs=[other.get(i, VMEM_SPEC) for i in range(len(args))],
            out_specs=jax.tree.map(lambda _: VMEM_SPEC, outs), scratch_shapes=scratch,
            compiler_params=pltpu.CompilerParams(vmem_limit_bytes=limit),
            cost_estimate=COST[name],
        )(*args)

    edge_shape = shape_of(HALF, 2 * MARGIN, BF16)
    to_left, to_right, mask = call(
        edges_kernel, (edge_shape, edge_shape, shape_of(TILE, TILE, F32)), {}, 4 << 20, (),
        "edges", mask_param,
    )
    from_right = move(to_left, 0, -1)
    from_left = move(to_right, 0, 1)
    goal_shape = shape_of(TILE, HALF, BF16)
    goal_left, goal_right, goal = call(
        goals_kernel, (goal_shape, goal_shape, shape_of(TILE, TILE, BF16)), {}, 4 << 20, (),
        "goals", target, to_right,
    )
    goal_right, goal_left = move(goal_left, 0, -1), move(goal_right, 0, 1)
    edge_table, weights = call(
        table_kernel, (shape_of(*EDGE_TABLE.shape, BF16), shape_of(KERN, COARSE, F32)), {},
        4 << 20, (), "table", edge_table, kernel_weight.reshape(1, KERN), to_right,
    )
    rim_shape = shape_of(MARGIN, 2 * MODES, BF16)
    half_spec, even_rim, odd_rim = call(
        lambda *refs: strip_kernel(cols, *refs),
        (shape_of(TILE, 2 * MODES, BF16), rim_shape, rim_shape), {}, 4 << 20, (), "strip",
        mask, from_left, from_right, edge_table,
    )
    goal_shape = shape_of(HALF, 2 * TILE, BF16)
    even_goal, odd_goal = call(
        goal_rows_kernel, (goal_shape, goal_shape), {}, 4 << 20, (), "goal_rows",
        goal, goal_left, goal_right, even_rim,
    )
    odd_rim = swap(odd_rim, 1)
    even_rim = swap(even_rim, 0)
    even_goal = swap(even_goal, 0)
    odd_goal = swap(odd_goal, 1)
    pair_shape = shape_of(2 * MODES, 2 * MODES, BF16)
    resp_shape = jax.ShapeDtypeStruct(kernel_modes.shape, F32)
    first, to_left, to_right, *responses = call(
        lambda *refs: first_kernel(rows, *refs),
        (shape_of(TILE, TILE, F32), pair_shape, pair_shape)
        + (resp_shape,) * 3,
        {}, 16 << 20, fields(1), "first", mask, half_spec, even_rim, odd_rim, goal, kernel_modes,
        weights, edge_table, table, level,
    )
    from_right = move(to_left, 0, -1)
    from_left = move(to_right, 0, 1)
    even_own, odd_own = call(
        lambda *refs: columns_kernel(cols, *refs), (pair_shape, pair_shape), {}, 4 << 20, (),
        "columns", to_left, to_right, from_left, from_right,
    )
    even_modes = swap(even_own, 0)
    odd_modes = swap(odd_own, 1)
    return call(
        lambda *refs: heal_kernel(rows, cols, *refs), shape_of(TILE, TILE, F32),
        {}, 24 << 20, fields(4), "heal",
        first, even_own, odd_own, even_modes, odd_modes, goal, goal_left,
        goal_right, even_goal, odd_goal, kernel_modes, *responses, weights, edge_table,
        table, level,
    )


def solution(mesh):
    rows, cols = mesh.shape["row"], mesh.shape["col"]
    tile = P(("grp", "row"), "col")

    def body(*args):
        return per_device(rows, cols, *args)

    return jax.shard_map(
        body, mesh=mesh, in_specs=(tile, tile, P(), P()), out_specs=tile, check_vma=False
    )
```

```python
import math

import jax
import jax.numpy as jnp
import numpy as np
from jax import lax
from jax.experimental import pallas as pl
from jax.experimental.pallas import tpu as pltpu
from jax.sharding import PartitionSpec as P


TILE = 256
MARGIN = 64
MODES = 64
KERN = 12
HALF = 128
WIN = 384
COARSE = 128
STEP = WIN // COARSE

threshold = 0.4
step_rate = 16.0
area = float(WIN * WIN)

VMEM = pltpu.VMEM
BF16 = jnp.bfloat16
F32 = jnp.float32


def tables():
    freq = np.arange(MODES) - MODES // 2
    angle = (2.0 * math.pi / WIN) * np.mod(freq[:, None] * np.arange(WIN)[None], WIN)
    cos, sin = np.cos(angle), np.sin(angle)
    stacked = np.concatenate([cos, sin], 0)
    forward = stacked.T
    core = slice(MARGIN, MARGIN + TILE)
    c_core, s_core = cos[:, core], sin[:, core]
    c_low, s_low = cos[:, ::STEP], sin[:, ::STEP]
    reach = HALF + MARGIN
    place_a = np.zeros((TILE, 2 * MODES))
    place_a[TILE - reach :] = forward[:reach]
    place_b = np.zeros((TILE, 2 * MODES))
    place_b[:reach] = forward[reach:]
    offset = np.arange(MARGIN, MARGIN + TILE)[:, None] - STEP * np.arange(COARSE)[None]
    orders = np.arange(1, 2 * MODES // 2)
    interp = 1.0 + 2.0 * np.cos((2.0 * math.pi / WIN) * orders[:, None, None] * offset[None]).sum(0)
    interp = (interp + np.cos((2.0 * math.pi / WIN) * MODES * offset)) / COARSE
    high = interp.astype(jnp.bfloat16).astype(np.float64)
    pad = np.zeros((COARSE, COARSE))
    table = dict(
        own=(forward[core], np.concatenate([c_core.T, -s_core.T], 1)),
        rim=(
            np.concatenate([forward[MARGIN + TILE :], forward[:MARGIN]], 0),
            np.concatenate([stacked[:, :MARGIN], stacked[:, MARGIN + TILE :]], 1),
        ),
        q_own=(stacked[:, core],),
        spread=(np.block([[c_low, s_low], [-s_low, c_low]]),),
        q_low=(np.concatenate([c_low.T, s_low.T], 1), pad),
        interp=(high, interp - high),
        interp_t=(np.concatenate([high.T, (interp - high).T], 0),),
        gather=(
            np.block(
                [[c_low.T, -s_low.T, -s_low.T, -c_low.T], [s_low.T, c_low.T, c_low.T, -s_low.T]]
            ),
        ),
        q_back=(c_low, s_low),
        inv_left=(np.block([[c_core[:, HALF:], s_core[:, HALF:]], [-s_core[:, HALF:], c_core[:, HALF:]]]),),
        inv_right=(np.block([[c_core[:, :HALF], s_core[:, :HALF]], [-s_core[:, :HALF], c_core[:, :HALF]]]),),
        place=(place_a, place_b),
        q_place=(np.concatenate([place_a.T, place_b.T], 0),),
    )
    table = {name: np.concatenate(value, 1) for name, value in table.items()}
    arrays, rows = [], {}
    for names in (("own", "rim"), tuple(name for name in table if name not in ("own", "rim"))):
        start = 0
        for name in names:
            rows[name] = slice(start, start + len(table[name]))
            start = rows[name].stop
        arrays.append(np.concatenate([table[name] for name in names], 0).astype(jnp.bfloat16))
    place = table["place"].astype(jnp.bfloat16).astype(np.float64)
    sums = 0.5 * place.sum(0)
    level = []
    for q in (place[:, : 2 * MODES].sum(0), place[:, 2 * MODES :].sum(0)):
        for t in (sums[: 2 * MODES], sums[2 * MODES :]):
            c, s = slice(0, MODES), slice(MODES, 2 * MODES)
            real = np.outer(q[c], t[c]) - np.outer(q[s], t[s])
            imag = -np.outer(q[c], t[s]) - np.outer(q[s], t[c])
            level.append(np.concatenate([real, imag], 1) / area)
    level.append(np.concatenate([sums.reshape(2, 2 * MODES), np.zeros((6, 2 * MODES))], 0))
    return arrays + [np.concatenate(level, 0).astype(np.float32)], rows


(EDGE_TABLE, MAIN_TABLE, LEVEL_TABLE), TABLE_ROWS = tables()


class Tables:
    def __init__(self, ref):
        self.ref = ref

    def __getitem__(self, name):
        return self.ref[TABLE_ROWS[name], :]

    def left(self, name):
        return self.ref[TABLE_ROWS[name], :COARSE]

    def right(self, name):
        return self.ref[TABLE_ROWS[name], COARSE:]


def dot(left, right):
    return jnp.dot(left, right, preferred_element_type=F32)


def swap_halves(value):
    return pltpu.roll(value, MODES, axis=1)


def low_lanes(shape):
    return lax.broadcasted_iota(jnp.int32, shape, 1) < MODES


def modes_of(blocks):
    top, bottom = blocks[:MODES], swap_halves(blocks[MODES:])
    return jnp.where(low_lanes(top.shape), top - bottom, -(top + bottom)) / area


def imaging_modes(windows, resp_ref, swapped_ref, scaled_ref, cross_ref, weight_ref, field_ref, t):
    count = len(windows)
    low = low_lanes((MODES, 2 * MODES))
    cuts = 2 if count == 1 else 1
    groups = [range(i * KERN // cuts, (i + 1) * KERN // cuts) for i in range(cuts)]
    partials = []
    for spec, _, _ in windows:
        swapped = swap_halves(spec)
        spec_a = jnp.where(low, spec, swapped)
        spec_b = jnp.where(low, -swapped, spec)
        partial = []
        for group in groups:
            filtered = [(resp_ref[k] * spec_a + swapped_ref[k] * spec_b).astype(BF16) for k in group]
            spread = dot(jnp.concatenate(filtered, 0), t["spread"]).astype(BF16)
            partial += [spread[i * MODES : (i + 1) * MODES] for i in range(len(group))]
        partials.append(partial)
    levels = []
    for w, partial in enumerate(partials):
        level = jnp.zeros((COARSE, COARSE), F32)
        for k, part in enumerate(partial):
            real, imag = part[:, :COARSE], part[:, COARSE:]
            rotated = jnp.concatenate([part, jnp.concatenate([-imag, real], 1)], 0)
            field = dot(t.left("q_low"), rotated)
            field_ref[w * KERN + k] = field
            a_real, a_imag = field[:, :COARSE], field[:, COARSE:]
            level = level + weight_ref[k : k + 1, :] * (a_real * a_real + a_imag * a_imag)
        levels.append((2.0 * level - 2.0 * threshold).astype(BF16))
    halves = [dot(t.left("interp"), level).astype(BF16) for level in levels]
    cores = [dot(half, t["interp_t"][:COARSE]) for half in halves]
    lows = []
    for core, (_, goal, inner) in zip(cores, windows):
        rise = jnp.tanh(core)
        core_grad = ((rise + (1.0 - 2.0 * goal.astype(F32))) * (1.0 - rise * rise)).astype(BF16)
        rows_low, cols_low = t["interp_t"][:COARSE], t.left("interp")
        inner_row, inner_col = inner
        if inner_row is not None:
            outer = jnp.where(inner_row, rows_low[:, HALF:].astype(F32), 0.0).astype(BF16)
            rows_low = jnp.concatenate([rows_low[:, :HALF], outer], 1)
        if inner_col is not None:
            outer = jnp.where(inner_col, cols_low[HALF:].astype(F32), 0.0).astype(BF16)
            cols_low = jnp.concatenate([cols_low[:HALF], outer], 0)
        lows.append((dot(rows_low, core_grad).astype(BF16), cols_low))
    lows = [dot(left, right) for left, right in lows]
    gathers = []
    for w, low_grad in enumerate(lows):
        both = jnp.concatenate([low_grad, low_grad], 1)
        gathered = []
        for group in groups:
            shaded = [(field_ref[w * KERN + k] * both).astype(BF16) for k in group]
            rows = dot(jnp.concatenate(shaded, 0), t["gather"]).astype(BF16)
            gathered += [rows[i * COARSE : (i + 1) * COARSE] for i in range(len(group))]
        gathers.append(gathered)
    results = []
    for gathered in gathers:
        direct = jnp.zeros((MODES, 2 * MODES), F32)
        crossed = jnp.zeros((MODES, 2 * MODES), F32)
        for k in range(0, KERN, 2):
            one, two = gathered[k], gathered[k + 1]
            upper = jnp.concatenate([one[:, :COARSE], two[:, :COARSE]], 1)
            lower = jnp.concatenate([one[:, COARSE:], two[:, COARSE:]], 1)
            back = dot(t["q_back"], jnp.concatenate([upper, lower], 0))
            for i, part in enumerate((back[:, : 2 * MODES], back[:, 2 * MODES :])):
                direct = direct + scaled_ref[k + i] * part
                crossed = crossed + cross_ref[k + i] * part
        results.append(
            jnp.where(low, direct + swap_halves(direct), crossed - swap_halves(crossed)).astype(BF16)
        )
    return results


def edges_kernel(mask_ref, left_ref, right_ref, mask_out_ref):
    low = low_lanes((TILE, 2 * MARGIN))
    edge = jax.nn.sigmoid(jnp.where(low, mask_ref[:, : 2 * MARGIN], mask_ref[:, HALF:]))
    top, bottom = edge[:HALF], edge[HALF:]
    low = low[:HALF]
    left_ref[...] = jnp.where(low, top, swap_halves(bottom)).astype(BF16)
    right_ref[...] = jnp.where(low, swap_halves(top), bottom).astype(BF16)
    mask_out_ref[...] = mask_ref[...]


def goals_kernel(target_ref, after_ref, left_ref, right_ref, target_out_ref):
    left_ref[...] = target_ref[:, :HALF]
    right_ref[...] = target_ref[:, HALF:]
    target_out_ref[...] = target_ref[...]


def table_kernel(table_ref, kernel_weight_ref, after_ref, out_ref, weight_ref):
    out_ref[...] = table_ref[...]
    weights = kernel_weight_ref[...]
    for k in range(KERN):
        weight_ref[k : k + 1, :] = jnp.broadcast_to(weights[:, k : k + 1], (1, COARSE))


def by_parity(odd, even_ref, odd_ref, below, above):
    @pl.when(odd)
    def _():
        even_ref[...] = above
        odd_ref[...] = below

    @pl.when(jnp.logical_not(odd))
    def _():
        even_ref[...] = below
        odd_ref[...] = above


def below_above(odd, even_ref, odd_ref):
    even, odd_value = even_ref[...].astype(F32), odd_ref[...].astype(F32)
    return jnp.where(odd, odd_value, even), jnp.where(odd, even, odd_value)


def strip_kernel(cols, mask_ref, left_ref, right_ref, table_ref, u_ref, even_ref, odd_ref):
    t = Tables(table_ref)
    col = lax.axis_index("col")
    odd = lax.rem(lax.axis_index("row"), 2) == 1
    wire = jax.nn.sigmoid(mask_ref[...]).astype(BF16)
    low = low_lanes((HALF, 2 * MARGIN))
    right = jnp.where(col < cols - 1, right_ref[...].astype(F32), 0.0)
    left = jnp.where(col > 0, left_ref[...].astype(F32), 0.0)
    rim = jnp.concatenate(
        [jnp.where(low, right, swap_halves(left)), jnp.where(low, swap_halves(right), left)], 0
    ).astype(BF16)
    half_spec = (dot(wire, t.left("own")) + dot(rim, t.left("rim"))).astype(BF16)
    u_ref[...] = half_spec
    by_parity(odd, even_ref, odd_ref, half_spec[TILE - MARGIN :], half_spec[:MARGIN])


def goal_rows_kernel(target_ref, left_ref, right_ref, after_ref, even_ref, odd_ref):
    odd = lax.rem(lax.axis_index("row"), 2) == 1
    goals = jnp.concatenate([left_ref[...], target_ref[...], right_ref[...]], 1)
    by_parity(odd, even_ref, odd_ref, goals[HALF:], goals[:HALF])


def first_kernel(
    rows, mask_ref, u_ref, even_ref, odd_ref, goal_ref, resp_ref, weight_ref,
    edge_table_ref, table_ref, level_ref, first_ref, left_ref, right_ref, swapped_ref, scaled_ref, cross_ref,
    field_ref,
):
    for k in range(KERN):
        weight = weight_ref[k : k + 1, :]
        swapped = swap_halves(resp_ref[k])
        swapped_ref[k] = swapped
        scaled_ref[k] = (2.0 * weight) * resp_ref[k]
        cross_ref[k] = (2.0 * weight) * swapped
    edge, t = Tables(edge_table_ref), Tables(table_ref)
    row = lax.axis_index("row")
    below, above = below_above(lax.rem(row, 2) == 1, even_ref, odd_ref)
    above = jnp.where(row > 0, above, 0.0)
    below = jnp.where(row < rows - 1, below, 0.0)
    rim = jnp.concatenate([above, below], 0).astype(BF16)
    spec = modes_of(dot(t["q_own"], u_ref[...]) + dot(edge.right("rim"), rim))
    (combined,) = imaging_modes(
        [(spec, goal_ref[...], (None, None))], resp_ref, swapped_ref, scaled_ref, cross_ref,
        weight_ref, field_ref, t,
    )
    left = dot(combined, t["inv_right"]).astype(BF16)
    right = dot(combined, t["inv_left"]).astype(BF16)
    real = jnp.concatenate([left[:, :HALF], right[:, :HALF]], 1)
    imag = jnp.concatenate([left[:, HALF:], right[:, HALF:]], 1)
    mask_grad = dot(edge.right("own"), jnp.concatenate([real, imag], 0))
    mask = mask_ref[...]
    first = updated(mask, mask_grad)
    first_ref[...] = first
    sums = jnp.concatenate([level_ref[4 * MODES : 4 * MODES + 1, :], level_ref[4 * MODES + 1 : 4 * MODES + 2, :]], 1)
    half = dot(jax.nn.sigmoid(first).astype(BF16), t["place"]) - sums
    blocks = dot(t["q_place"], half.astype(BF16))
    right_ref[:MODES, :] = modes_of(blocks[:HALF, :HALF]).astype(BF16)
    left_ref[:MODES, :] = modes_of(blocks[:HALF, HALF:]).astype(BF16)
    right_ref[MODES:, :] = modes_of(blocks[HALF:, :HALF]).astype(BF16)
    left_ref[MODES:, :] = modes_of(blocks[HALF:, HALF:]).astype(BF16)


def updated(param, grad):
    rise = jnp.tanh(0.5 * param)
    return param - (step_rate / 4.0 / area) * (grad * (1.0 - rise * rise))


def columns_kernel(cols, own_left_ref, own_right_ref, left_ref, right_ref, even_ref, odd_ref):
    col = lax.axis_index("col")
    odd = lax.rem(lax.axis_index("row"), 2) == 1
    own = own_right_ref[...].astype(F32) + jnp.where(col < cols - 1, right_ref[...].astype(F32), 0.0)
    before = own_left_ref[...].astype(F32) + jnp.where(col > 0, left_ref[...].astype(F32), 0.0)
    below = jnp.concatenate([own[:MODES], before[:MODES]], 0).astype(BF16)
    above = jnp.concatenate([own[MODES:], before[MODES:]], 0).astype(BF16)
    by_parity(odd, even_ref, odd_ref, below, above)


def heal_kernel(
    rows, cols, first_ref, even_own_ref, odd_own_ref, even_ref, odd_ref, goal_ref, left_ref,
    right_ref, even_goal_ref, odd_goal_ref, resp_ref, swapped_ref, scaled_ref, cross_ref,
    weight_ref, edge_table_ref, table_ref, level_ref, out_ref, field_ref,
):
    edge, t = Tables(edge_table_ref), Tables(table_ref)
    row, col = lax.axis_index("row"), lax.axis_index("col")
    odd = lax.rem(row, 2) == 1
    inner_row, inner_col = row < rows - 1, col < cols - 1
    lower, upper = below_above(odd, even_own_ref, odd_own_ref)
    below, above = below_above(odd, even_ref, odd_ref)
    lower = lower + jnp.where(inner_row, below, 0.0)
    upper = upper + jnp.where(row > 0, above, 0.0)
    aa, ab, ba, bb = (level_ref[i * MODES : (i + 1) * MODES, :] for i in range(4))
    own_columns = aa + jnp.where(inner_col, ab, 0.0), ba + jnp.where(inner_col, bb, 0.0)
    both_columns = aa + ab, ba + bb
    lower = lower + jnp.concatenate(
        [a + jnp.where(inner_row, b, 0.0) for a, b in (own_columns, both_columns)], 0
    )
    upper = upper + jnp.concatenate([a + b for a, b in (own_columns, both_columns)], 0)
    own_goals = jnp.concatenate([left_ref[...], goal_ref[...], right_ref[...]], 1)
    goals_below, goals_above = below_above(odd, even_goal_ref, odd_goal_ref)
    goals_lower = jnp.concatenate([own_goals[HALF:].astype(F32), goals_below], 0)
    goals_upper = jnp.concatenate([goals_above, own_goals[:HALF].astype(F32)], 0)
    lower_right, lower_left, upper_right, upper_left = imaging_modes(
        [
            (lower[:MODES], goals_lower[:, TILE:], (inner_row, inner_col)),
            (lower[MODES:], goals_lower[:, :TILE], (inner_row, None)),
            (upper[:MODES], goals_upper[:, TILE:], (None, inner_col)),
            (upper[MODES:], goals_upper[:, :TILE], (None, None)),
        ],
        resp_ref, swapped_ref, scaled_ref, cross_ref, weight_ref, field_ref, t,
    )

    def kept(value, flag):
        return jnp.where(flag, value.astype(F32), 0.0).astype(BF16)

    left = jnp.concatenate(
        [kept(lower_left, col > 0), kept(upper_left, jnp.logical_and(row > 0, col > 0))], 0
    )
    right = jnp.concatenate([lower_right, kept(upper_right, row > 0)], 0)
    left = dot(left, t["inv_left"]).astype(BF16)
    right = dot(right, t["inv_right"]).astype(BF16)

    def quarter(modes):
        real = jnp.concatenate([left[modes, :HALF], right[modes, :HALF]], 1)
        imag = jnp.concatenate([left[modes, HALF:], right[modes, HALF:]], 1)
        return jnp.concatenate([real, imag], 0)

    q_inv = edge.right("own")
    below = dot(q_inv[:HALF], quarter(slice(0, MODES)))
    above = dot(q_inv[HALF:], quarter(slice(MODES, 2 * MODES)))
    out_ref[:HALF, :] = updated(first_ref[:HALF, :], above)
    out_ref[HALF:, :] = updated(first_ref[HALF:, :], below)


COST = {
    name: pl.CostEstimate(flops=int(micros * 1.1e9), bytes_accessed=1 << 16, transcendentals=0)
    for name, micros in (
        ("edges", 1.0), ("goals", 1.0), ("table", 1.0), ("strip", 1.0), ("goal_rows", 1.0),
        ("first", 3.0), ("columns", 1.0), ("heal", 5.0),
    )
}
VMEM_SPEC = pl.BlockSpec(memory_space=VMEM)
SMEM_SPEC = pl.BlockSpec(memory_space=pltpu.SMEM)


def fields(windows):
    return [VMEM((windows * KERN, COARSE, 2 * COARSE), F32)]


def shape_of(rows, cols, dtype):
    return jax.ShapeDtypeStruct((rows, cols), dtype)


def per_device(rows, cols, mask_param, target, kernel_modes, kernel_weight):
    table, edge_table = jnp.asarray(MAIN_TABLE), jnp.asarray(EDGE_TABLE)
    level = jnp.asarray(LEVEL_TABLE)

    def permuted(value, place):
        pairs = [
            (r * cols + c, place(r, c)[0] * cols + place(r, c)[1])
            for r in range(rows)
            for c in range(cols)
        ]
        return lax.ppermute(value, ("row", "col"), pairs)

    def move(value, down, right):
        return permuted(value, lambda r, c: ((r + down) % rows, (c + right) % cols))

    def swap(value, parity):
        def place(r, c):
            other = r + 1 if r % 2 == parity else r - 1
            return (other, c) if 0 <= other < rows else (r, c ^ 1)

        return permuted(value, place)

    def call(kernel, outs, other, limit, scratch, name, *args):
        return pl.pallas_call(
            kernel, out_shape=outs, in_specs=[other.get(i, VMEM_SPEC) for i in range(len(args))],
            out_specs=jax.tree.map(lambda _: VMEM_SPEC, outs), scratch_shapes=scratch,
            compiler_params=pltpu.CompilerParams(vmem_limit_bytes=limit),
            cost_estimate=COST[name],
        )(*args)

    edge_shape = shape_of(HALF, 2 * MARGIN, BF16)
    to_left, to_right, mask = call(
        edges_kernel, (edge_shape, edge_shape, shape_of(TILE, TILE, F32)), {}, 4 << 20, (),
        "edges", mask_param,
    )
    from_right = move(to_left, 0, -1)
    from_left = move(to_right, 0, 1)
    goal_shape = shape_of(TILE, HALF, BF16)
    goal_left, goal_right, goal = call(
        goals_kernel, (goal_shape, goal_shape, shape_of(TILE, TILE, BF16)), {}, 4 << 20, (),
        "goals", target, to_right,
    )
    goal_right, goal_left = move(goal_left, 0, -1), move(goal_right, 0, 1)
    edge_table, weights = call(
        table_kernel, (shape_of(*EDGE_TABLE.shape, BF16), shape_of(KERN, COARSE, F32)), {},
        4 << 20, (), "table", edge_table, kernel_weight.reshape(1, KERN), to_right,
    )
    rim_shape = shape_of(MARGIN, 2 * MODES, BF16)
    half_spec, even_rim, odd_rim = call(
        lambda *refs: strip_kernel(cols, *refs),
        (shape_of(TILE, 2 * MODES, BF16), rim_shape, rim_shape), {}, 4 << 20, (), "strip",
        mask, from_left, from_right, edge_table,
    )
    goal_shape = shape_of(HALF, 2 * TILE, BF16)
    even_goal, odd_goal = call(
        goal_rows_kernel, (goal_shape, goal_shape), {}, 4 << 20, (), "goal_rows",
        goal, goal_left, goal_right, even_rim,
    )
    odd_rim = swap(odd_rim, 1)
    even_rim = swap(even_rim, 0)
    even_goal = swap(even_goal, 0)
    odd_goal = swap(odd_goal, 1)
    pair_shape = shape_of(2 * MODES, 2 * MODES, BF16)
    resp_shape = jax.ShapeDtypeStruct(kernel_modes.shape, F32)
    first, to_left, to_right, *responses = call(
        lambda *refs: first_kernel(rows, *refs),
        (shape_of(TILE, TILE, F32), pair_shape, pair_shape)
        + (resp_shape,) * 3,
        {}, 16 << 20, fields(1), "first", mask, half_spec, even_rim, odd_rim, goal, kernel_modes,
        weights, edge_table, table, level,
    )
    from_right = move(to_left, 0, -1)
    from_left = move(to_right, 0, 1)
    even_own, odd_own = call(
        lambda *refs: columns_kernel(cols, *refs), (pair_shape, pair_shape), {}, 4 << 20, (),
        "columns", to_left, to_right, from_left, from_right,
    )
    even_modes = swap(even_own, 0)
    odd_modes = swap(odd_own, 1)
    return call(
        lambda *refs: heal_kernel(rows, cols, *refs), shape_of(TILE, TILE, F32),
        {}, 24 << 20, fields(4), "heal",
        first, even_own, odd_own, even_modes, odd_modes, goal, goal_left,
        goal_right, even_goal, odd_goal, kernel_modes, *responses, weights, edge_table,
        table, level,
    )


def solution(mesh):
    rows, cols = mesh.shape["row"], mesh.shape["col"]
    tile = P(("grp", "row"), "col")

    def body(*args):
        return per_device(rows, cols, *args)

    return jax.shard_map(
        body, mesh=mesh, in_specs=(tile, tile, P(), P()), out_specs=tile, check_vma=False
    )
```
